512 devices in a mesh: fsdp: 16 (over z_hi, x, core), seq: 32 (over z_lo, y).
Axes of the slice: x: 4, y: 4, z: 16 (z_hi: 2, z_lo: 8; z = z_hi * 8 + z_lo), core: 2. Of those that a mesh axis runs over, the one named last changes fastest.
Arguments:
- qkv: bfloat16 [16, 4096, 6144], P('fsdp', 'seq'), may hold values from -128 to 128
- resid: bfloat16 [16, 4096, 2048], P('fsdp', 'seq'), may hold values from -0.625 to 0.625
- earlier: float32 [16, 4096, 2048], P('fsdp', 'seq'), may hold values from -12 to 12
- lengths: int32 [16, 12], P('fsdp'), may hold values from 1 to 512, 4096 in all within a row
- teacher_out: bfloat16 [2048, 2048], P('seq', 'fsdp'), may hold values from -6 to 6
- student_out: bfloat16 [2048, 2048], P('seq', 'fsdp'), may hold values from -6 to 6
Outputs:
- targets: float32 [16, 4096, 2048], P('fsdp', 'seq')
- teacher_new: bfloat16 [2048, 2048], P('seq', 'fsdp')
The draws below stay inside these ranges and needn't reach their ends.
Inputs may be any that keep to these rules, and one draw needn't show every extreme that they name: Each pack's 12 utterance lengths add up to its 4096 frames, and one of them is exactly 512.
All inputs are finite; a program needn't handle non-finite values.
Results may differ from the reference program's by a relative error of at most 0.0019.
Values may be sent and summed in bfloat16 or wider, within the bound.
No kernel may reach another device: no remote copies, remote signals or barrier semaphores. Data moves between devices by JAX's collectives and lax.ppermute only.
A program may use at most 64 MiB of HBM per device.

```python
import math
import jax
import jax.numpy as jnp
import numpy as np
from jax import lax

D = 2048
HEADS = 32
HEAD_DIM = 64
TOP_K = 8
UTTS = 12
FRAMES = 4096
UTT_MAX = 512
PACKS = 16


def draw_qkv(key, part):
    keys_list = jax.random.split(key, 1)
    shape_full = (PACKS, FRAMES, 3, HEADS, HEAD_DIM)
    values_base = jax.random.normal(keys_list[0], shape_full, jnp.float32)
    return values_base.reshape(PACKS, FRAMES, 3 * D).astype(jnp.bfloat16)


def level_of(rng, extent, cuts, low, top_value):
    def one(dim, parts):
        steps = jax.random.uniform(jax.random.fold_in(jax.random.fold_in(rng, 6), dim), (parts,), jnp.float32, low / len(cuts), top_value / len(cuts))
        return jnp.repeat(jnp.exp(steps), extent[dim] // parts).reshape((-1,) + (1,) * (len(extent) - dim - 1))

    gain = one(*cuts[0])
    for cut in cuts[1:]:
        gain = gain * one(*cut)
    return gain


def profile(number_of, total, limit, skew):
    weights = [(1 << 20) // math.isqrt(rank ** skew) + 1 for rank in range(2, number_of + 1)]
    spare, given = total - limit - (number_of - 1), [1] * (number_of - 1)
    while spare > 0:
        free = [i for i in range(number_of - 1) if given[i] < limit]
        pool, budget = sum([weights[i] for i in free]), spare
        for i in free:
            more = min(limit - given[i], max(1, budget * weights[i] // pool), spare)
            given[i] = given[i] + more
            spare = spare - more
    return np.array([limit] + given)


def ragged(key, count, total, most, slope):
    if count == 2:
        one = jax.random.randint(key, (), max(1, total - most), min(most, total - 1) + 1)
        return jnp.stack([one, total - one])
    tallies = jnp.asarray(profile(count, total, most, slope), jnp.int32)
    twos = (count - 1) // 2
    donor, receiver = tallies[1:1 + 2 * twos:2], tallies[2:2 + 2 * twos:2]
    margin = jnp.minimum(donor - 1, most - receiver)
    moved = jax.random.randint(jax.random.fold_in(key, 1), (twos,), 0, 1 << 20) % (margin + 1)
    tallies = tallies.at[1:1 + 2 * twos:2].set(donor - moved).at[2:2 + 2 * twos:2].set(receiver + moved)
    return tallies[jax.random.permutation(jax.random.fold_in(key, 2), count)]


def gaussian(own_key, shape, deviation, bound, cuts=(), held_as=jnp.bfloat16):
    array = deviation * jax.random.normal(own_key, shape, jnp.float32)
    if cuts:
        array = array * level_of(own_key, shape, cuts, -0.22, 0.18)
    return jnp.clip(array, -bound, bound).astype(held_as)


def setup_inputs(seed: int = 0) -> dict:
    arg_keys = jax.random.split(jax.random.key(seed), 7)
    qkv = draw_qkv(jax.random.fold_in(arg_keys[6], 71), 0)
    resid = gaussian(arg_keys[1], (PACKS, FRAMES, D), 0.1, 0.625, ((0, 16), (1, 32)))
    earlier = gaussian(arg_keys[2], (PACKS, FRAMES, D), 2.0, 12.0, ((0, 16), (1, 32)), jnp.float32)
    lengths = jax.vmap(lambda own: ragged(own, UTTS, FRAMES, UTT_MAX, 1))(jax.random.split(arg_keys[3], PACKS)).reshape((PACKS, UTTS)).astype(jnp.int32)
    teacher_out = gaussian(arg_keys[4], (D, D), 1.0, 6.0, ((0, 32), (1, 16)))
    student_out = gaussian(arg_keys[5], (D, D), 1.0, 6.0, ((0, 32), (1, 16)))
    return dict(qkv=qkv, resid=resid, earlier=earlier, lengths=lengths, teacher_out=teacher_out, student_out=student_out)


ema_decay = 0.9
norm_epsilon = 1e-05
masked_score = -1e+30

def segment_ids(utt_lengths, frames):
    utt_ends = jnp.cumsum(utt_lengths).astype(jnp.int32)
    places = jnp.arange(frames, dtype=jnp.int32)
    return lax.optimization_barrier(jnp.sum((places[:, None] >= utt_ends[None, :]).astype(jnp.int32), axis=1))

def attend_dense(stacked, segment):
    inverse_root = 1.0 / math.sqrt(stacked.shape[-1])
    moved = jnp.transpose(stacked.astype(jnp.float32), (2, 1, 0, 3))
    allowed = segment[:, None] == segment[None, :]

    def one_head(head_rows):
        scores = jnp.dot(head_rows[0], head_rows[1].T, precision=lax.Precision.HIGHEST) * inverse_root
        scores = jnp.where(allowed, scores, masked_score)
        row_max = lax.optimization_barrier(jnp.max(scores, axis=1, keepdims=True))
        weights = jnp.exp(scores - row_max)
        row_total = lax.optimization_barrier(jnp.sum(weights, axis=1, keepdims=True))
        rounded = lax.optimization_barrier(weights.astype(jnp.bfloat16)).astype(jnp.float32)
        summed = jnp.dot(rounded, head_rows[2], precision=lax.Precision.HIGHEST)
        return (summed / row_total).astype(jnp.bfloat16)
    outputs = lax.map(one_head, moved)
    return jnp.transpose(outputs, (1, 0, 2)).reshape(stacked.shape[0], -1)

def reference(qkv, resid, earlier, lengths, teacher_out, student_out):
    teacher_new = (ema_decay * teacher_out.astype(jnp.float32) + (1.0 - ema_decay) * student_out.astype(jnp.float32)).astype(jnp.bfloat16)

    def one_pack(pack_args):
        pack_qkv, pack_resid, pack_earlier, pack_lengths = pack_args
        segment = segment_ids(pack_lengths, FRAMES)
        stacked = pack_qkv.reshape(FRAMES, 3, HEADS, HEAD_DIM)
        mixed = attend_dense(stacked, segment)
        branch = jnp.dot(mixed, teacher_new, preferred_element_type=jnp.float32) / math.sqrt(D)
        summed = pack_resid.astype(jnp.float32) + branch
        centered = summed - lax.optimization_barrier(jnp.mean(summed, axis=1, keepdims=True))
        normed = centered * lax.rsqrt(lax.optimization_barrier(jnp.mean(centered * centered, axis=1, keepdims=True)) + norm_epsilon)
        return (pack_earlier + normed) / TOP_K
    targets = lax.map(one_pack, (qkv, resid, earlier, lengths))
    return (targets, teacher_new)
```

```python
import functools
import math

import jax
import jax.numpy as jnp
from jax import lax
from jax.experimental import pallas as pl
from jax.experimental.pallas import tpu as pltpu
from jax.sharding import Mesh, PartitionSpec as P

D = 2048
HEADS = 32
HEAD_DIM = 64
TOP_K = 8
UTTS = 12
LANES = 128
TOKENS = 128
ROW = 512
WIDTH = 512
CHUNK = 256
PAIRS = WIDTH // LANES

ema_decay = 0.9
norm_epsilon = 1e-05
masked_score = -1e30


def pack_kernel(qkv_ref, kv_ref, q_ref):
    low = lax.broadcasted_iota(jnp.int32, (TOKENS, LANES), 1) < HEAD_DIM
    for part in range(3):
        for pair in range(PAIRS):
            for half in range(2):
                base = part * D + pair * 512 + half * LANES
                first = qkv_ref[:, base : base + LANES]
                second = qkv_ref[:, base + 256 : base + 256 + LANES]
                turned_first = pltpu.roll(first.astype(jnp.float32), HEAD_DIM, 1).astype(jnp.bfloat16)
                turned_second = pltpu.roll(second.astype(jnp.float32), HEAD_DIM, 1).astype(jnp.bfloat16)
                even = jnp.where(low, first, turned_second)
                odd = jnp.where(low, turned_first, second)
                lanes = slice(pair * LANES, (pair + 1) * LANES)
                if part == 0:
                    inverse_root = 1.0 / math.sqrt(HEAD_DIM)
                    q_ref[2 * half, :, lanes] = (even * inverse_root).astype(jnp.bfloat16)
                    q_ref[2 * half + 1, :, lanes] = (odd * inverse_root).astype(jnp.bfloat16)
                else:
                    start = (part - 1) * WIDTH + pair * LANES
                    lanes = slice(start, start + LANES)
                    kv_ref[2 * half, :, lanes] = even
                    kv_ref[2 * half + 1, :, lanes] = odd


def attend_kernel(
    lengths_ref, place_ref, q_ref, before_ref, own_ref, after_ref, out_ref,
    kv, scores, tops, totals, sums, sems,
):
    copies = [
        pltpu.make_async_copy(source, kv.at[pl.ds(i * ROW, ROW)], sems.at[i])
        for i, source in enumerate((before_ref, own_ref, after_ref))
    ]
    for copy in copies:
        copy.start()
    kv[3 * ROW :, :] = jnp.zeros((LANES, 2 * WIDTH), jnp.bfloat16)
    row_start = place_ref[0] * ROW
    y = place_ref[1]
    base = row_start - ROW
    ends = []
    total = jnp.int32(0)
    for j in range(UTTS):
        total = total + lengths_ref[0, j]
        ends.append(total)

    def segments(frames):
        found = jnp.zeros(frames.shape, jnp.int32)
        for end in ends:
            found = found + (frames >= end).astype(jnp.int32)
        return jnp.where(frames < 0, -1, found)

    for copy in copies:
        copy.wait()
    low = lax.broadcasted_iota(jnp.int32, (TOKENS, LANES), 1) < HEAD_DIM

    def block(turn, carry):
        which = lax.rem(y + 1 + turn, 4)
        first = row_start + which * TOKENS
        last = first + TOKENS - 1
        begin = jnp.int32(0)
        finish = jnp.int32(0)
        for end in reversed(ends):
            finish = jnp.where(end > last, end, finish)
        for end in ends:
            begin = jnp.where(end <= first, end, begin)
        key_block = lax.div(begin - base, LANES)
        steps = lax.div(finish - base - key_block * LANES + CHUNK - 1, CHUNK)
        row_segment = segments(
            first + lax.broadcasted_iota(jnp.int32, (TOKENS, LANES), 0)
        )
        row_segment = jnp.concatenate([row_segment, row_segment], axis=1)
        queries = []
        for pair in range(PAIRS):
            one = q_ref[pl.ds(pl.multiple_of(which * TOKENS, TOKENS), TOKENS), pair * LANES : (pair + 1) * LANES]
            zero = jnp.zeros_like(one)
            queries.append(
                jnp.concatenate([jnp.where(low, one, zero), jnp.where(low, zero, one)], axis=0)
            )
        tops[...] = jnp.full(tops.shape, masked_score, jnp.float32)
        totals[...] = jnp.zeros(totals.shape, jnp.float32)
        sums[...] = jnp.zeros(sums.shape, jnp.float32)

        def score(step, carry):
            start = pl.multiple_of(key_block * LANES + step * CHUNK, LANES)
            key_segment = segments(
                base + start + lax.broadcasted_iota(jnp.int32, (8, CHUNK), 1)
            )[:1]
            allowed = row_segment == key_segment
            allowed = jnp.concatenate([allowed, allowed], axis=0)
            for pair in range(PAIRS):
                keys = kv[pl.ds(start, CHUNK), pair * LANES : (pair + 1) * LANES]
                found = lax.dot_general(
                    queries[pair], keys, (((1,), (1,)), ((), ())),
                    preferred_element_type=jnp.float32,
                )
                found = jnp.where(allowed, found, masked_score)
                scores[step, pair] = found
                tops[pair] = jnp.maximum(
                    tops[pair], jnp.maximum(found[:, :LANES], found[:, LANES:])
                )
            return carry

        lax.fori_loop(0, steps, score, 0)
        for pair in range(PAIRS):
            top = jnp.max(tops[pair], axis=1, keepdims=True)
            tops[pair] = jnp.broadcast_to(top, (2 * TOKENS, LANES))

        def mix(step, carry):
            start = pl.multiple_of(key_block * LANES + step * CHUNK, LANES)
            for pair in range(PAIRS):
                found = scores[step, pair]
                left = jnp.exp(found[:, :LANES] - tops[pair])
                right = jnp.exp(found[:, LANES:] - tops[pair])
                totals[pair] = totals[pair] + (left + right)
                weights = jnp.concatenate([left, right], axis=1).astype(jnp.bfloat16)
                values = kv[
                    pl.ds(start, CHUNK), WIDTH + pair * LANES : WIDTH + (pair + 1) * LANES
                ]
                sums[pair] = sums[pair] + jnp.dot(
                    weights, values, preferred_element_type=jnp.float32
                )
            return carry

        lax.fori_loop(0, steps, mix, 0)
        for pair in range(PAIRS):
            row_total = jnp.sum(totals[pair], axis=1, keepdims=True)
            mixed = sums[pair] / row_total
            out_ref[turn, :, pair * LANES : (pair + 1) * LANES] = jnp.where(
                low, mixed[:TOKENS], mixed[TOKENS:]
            ).astype(jnp.bfloat16)
        return carry

    lax.fori_loop(0, 4, block, 0)


def project(mixed, weights_ref, store):
    for tile in range(0, 16, 2):
        high, place = divmod(tile, 8)
        both = jnp.concatenate(
            [weights_ref[2 * place + high], weights_ref[2 * (place + 1) + high]], axis=1
        )
        store(tile * LANES, jnp.dot(mixed, both, preferred_element_type=jnp.float32))


def partial_kernel(mixed_ref, weights_ref, out_ref):
    def store(start, value):
        out_ref[:, start : start + 2 * LANES] = value.astype(jnp.bfloat16)

    project(mixed_ref[...], weights_ref, store)


def own_kernel(mixed_ref, weights_ref, resid_ref, out_ref):
    def store(start, value):
        span = slice(start, start + 2 * LANES)
        out_ref[:, span] = value

    project(mixed_ref[...], weights_ref, store)


def finish_kernel(own_ref, one_ref, two_ref, three_ref, resid_ref, earlier_ref, out_ref):
    branch = own_ref[...] + one_ref[...].astype(jnp.float32)
    branch = branch + two_ref[...].astype(jnp.float32)
    branch = branch + three_ref[...].astype(jnp.float32)
    summed = resid_ref[...].astype(jnp.float32) + branch * (1.0 / math.sqrt(D))
    centered = summed - jnp.mean(summed, axis=1, keepdims=True)
    spread = jnp.mean(centered * centered, axis=1, keepdims=True)
    normed = centered * lax.rsqrt(spread + norm_epsilon)
    out_ref[...] = (earlier_ref[...] + normed) * (1.0 / TOP_K)


vmem = pl.BlockSpec(memory_space=pltpu.VMEM)
smem = pl.BlockSpec(memory_space=pltpu.SMEM)
anywhere = pl.BlockSpec(memory_space=pl.ANY)


def cost(flops, moved, exps=0):
    return pl.CostEstimate(flops=flops, bytes_accessed=moved, transcendentals=exps)


def shards(qkv, resid, earlier, lengths, teacher_out, student_out):
    teacher_new = (
        ema_decay * teacher_out.astype(jnp.float32)
        + (1.0 - ema_decay) * student_out.astype(jnp.float32)
    ).astype(jnp.bfloat16)
    place = jnp.stack([lax.axis_index("z"), lax.axis_index("y")]).astype(jnp.int32)

    kv, q = pl.pallas_call(
        pack_kernel,
        out_shape=(
            jax.ShapeDtypeStruct((4, TOKENS, 2 * WIDTH), jnp.bfloat16),
            jax.ShapeDtypeStruct((4, TOKENS, WIDTH), jnp.bfloat16),
        ),
        in_specs=[vmem],
        out_specs=(vmem, vmem),
        cost_estimate=cost(0, 3 << 20),
        name="pack",
    )(qkv[0])

    kv_row = lax.all_to_all(kv, "y", 0, 0, tiled=True)
    ring = 2 * lax.axis_size("z")
    after = lax.ppermute(kv_row, ("h", "z"), [((i + 1) % ring, i) for i in range(ring)])
    before = lax.ppermute(kv_row, ("h", "z"), [(i, (i + 1) % ring) for i in range(ring)])
    q_row = lax.all_to_all(q, "y", 0, 0, tiled=True)

    ring_weights = lax.all_to_all(
        jnp.broadcast_to(teacher_new[None], (16,) + teacher_new.shape), ("h", "z"), 0, 0, tiled=True
    )
    weights = lax.all_to_all(
        jnp.broadcast_to(ring_weights[None], (8,) + ring_weights.shape), ("x", "c"), 0, 0, tiled=True
    )
    weights = weights.reshape(16, ROW, LANES)

    mixed = pl.pallas_call(
        attend_kernel,
        out_shape=jax.ShapeDtypeStruct((4, TOKENS, WIDTH), jnp.bfloat16),
        in_specs=[smem, smem, vmem, anywhere, anywhere, anywhere],
        out_specs=vmem,
        scratch_shapes=[
            pltpu.VMEM((3 * ROW + LANES, 2 * WIDTH), jnp.bfloat16),
            pltpu.VMEM((6, PAIRS, 2 * TOKENS, CHUNK), jnp.float32),
            pltpu.VMEM((PAIRS, 2 * TOKENS, LANES), jnp.float32),
            pltpu.VMEM((PAIRS, 2 * TOKENS, LANES), jnp.float32),
            pltpu.VMEM((PAIRS, 2 * TOKENS, LANES), jnp.float32),
            pltpu.SemaphoreType.DMA((3,)),
        ],
        cost_estimate=cost(2 << 30, 4 << 20, 4 << 20),
        name="attend",
    )(
        lengths, place, q_row.reshape(ROW, WIDTH),
        before.reshape(ROW, 2 * WIDTH), kv_row.reshape(ROW, 2 * WIDTH), after.reshape(ROW, 2 * WIDTH),
    )

    arrived = []
    for turn in range(3):
        part = pl.pallas_call(
            partial_kernel,
            out_shape=jax.ShapeDtypeStruct((TOKENS, D), jnp.bfloat16),
            in_specs=[vmem, vmem],
            out_specs=vmem,
            cost_estimate=cost(2 * TOKENS * WIDTH * D, 3 << 20),
            name="partial",
        )(mixed[turn], weights)
        arrived.append(
            lax.ppermute(part, "y", [(i, (i + 1 + turn) % 4) for i in range(4)])
        )
    own = pl.pallas_call(
        own_kernel,
        out_shape=jax.ShapeDtypeStruct((TOKENS, D), jnp.float32),
        in_specs=[vmem, vmem, vmem],
        out_specs=vmem,
        cost_estimate=cost(2 * TOKENS * WIDTH * D, 3 << 20),
        name="own",
    )(mixed[3], weights, resid[0])
    targets = pl.pallas_call(
        finish_kernel,
        out_shape=jax.ShapeDtypeStruct((TOKENS, D), jnp.float32),
        in_specs=[vmem] * 6,
        out_specs=vmem,
        cost_estimate=cost(1 << 22, 5 << 20),
        name="finish",
    )(own, *arrived, resid[0], earlier[0])
    return (targets[None], teacher_new)


def solution(mesh):
    fine = Mesh(
        mesh.devices.reshape(2, 4, 2, 8, 4), ("h", "x", "c", "z", "y")
    )
    packs, frames = ("h", "x", "c"), ("z", "y")
    placed = (
        P(packs, frames, None),
        P(packs, frames, None),
        P(packs, frames, None),
        P(packs, None),
        P(frames, packs),
        P(frames, packs),
    )
    return jax.shard_map(
        shards,
        mesh=fine,
        in_specs=placed,
        out_specs=(P(packs, frames, None), P(frames, packs)),
        check_vma=False,
    )
```

```python
import functools
import math

import jax
import jax.numpy as jnp
from jax import lax
from jax.experimental import pallas as pl
from jax.experimental.pallas import tpu as pltpu
from jax.sharding import Mesh, PartitionSpec as P

D = 2048
HEAD_DIM = 64
TOP_K = 8
UTTS = 12
LANES = 128
TOKENS = 128
ROW = 512
WIDTH = 512
CHUNK = 256
PAIRS = WIDTH // LANES
PACKED = 32

ema_decay = 0.9
norm_epsilon = 1e-05
masked_score = -1e30


def pack_kernel(place_ref, qkv_ref, *outs):
    y = place_ref[1]
    low = lax.broadcasted_iota(jnp.int32, (PACKED, LANES), 1) < HEAD_DIM
    for turn in range(4):
        target = lax.rem(y + 4 - turn, 4)
        odd = lax.rem(target, 2) == 1
        half = lax.div(target, 2) * LANES
        for part in range(3):
            for pair in range(PAIRS):
                base = part * D + pair * 512
                first = qkv_ref[:, pl.ds(pl.multiple_of(base + half, LANES), LANES)].astype(jnp.float32)
                second = qkv_ref[:, pl.ds(pl.multiple_of(base + 256 + half, LANES), LANES)].astype(jnp.float32)
                left = jnp.where(odd, pltpu.roll(first, HEAD_DIM, 1), first)
                right = jnp.where(odd, second, pltpu.roll(second, HEAD_DIM, 1))
                both = jnp.where(low, left, right)
                if part == 0:
                    both = both * (1.0 / math.sqrt(HEAD_DIM))
                    outs[4 + turn][:, pair * LANES : (pair + 1) * LANES] = both.astype(jnp.bfloat16)
                else:
                    start = (part - 1) * WIDTH + pair * LANES
                    outs[turn][:, start : start + LANES] = both.astype(jnp.bfloat16)


class Attention:
    def __init__(self, lengths_ref, place_ref, sources, kv, scores, tops, totals, sums, sems):
        self.kv, self.scores, self.tops, self.totals, self.sums = kv, scores, tops, totals, sums
        self.row_start = place_ref[0] * ROW
        self.y = place_ref[1]
        self.base = self.row_start - ROW
        self.ends = []
        total = jnp.int32(0)
        for j in range(UTTS):
            total = total + lengths_ref[0, j]
            self.ends.append(total)
        self.low = lax.broadcasted_iota(jnp.int32, (TOKENS, LANES), 1) < HEAD_DIM
        self.copies = []
        for turn in range(4):
            slot = lax.rem(self.y + turn, 4)
            views = [sources[turn]]
            for side in range(2):
                own, rest = sources[4 + 2 * side], sources[5 + 2 * side]
                views.append(own if turn == 0 else rest.at[pl.ds((turn - 1) * TOKENS, TOKENS)])
            for view, row in zip(views, (1, 0, 2)):
                where = slot + 4 * row
                target = kv.at[pl.ds(pl.multiple_of(where * TOKENS, TOKENS), TOKENS)]
                self.copies.append(
                    (where, pltpu.make_async_copy(view, target, sems.at[len(self.copies)]))
                )

    def keys_of(self, which):
        first = self.row_start + which * TOKENS
        last = first + TOKENS - 1
        begin = jnp.int32(0)
        finish = jnp.int32(0)
        for end in reversed(self.ends):
            finish = jnp.where(end > last, end, finish)
        for end in self.ends:
            begin = jnp.where(end <= first, end, begin)
        start = lax.div(begin - self.base, TOKENS)
        stop = lax.div(finish - self.base + TOKENS - 1, TOKENS)
        return start, stop

    def load(self, blocks):
        ranges = [self.keys_of(which) for which in blocks]
        start = functools.reduce(jnp.minimum, [r[0] for r in ranges])
        stop = functools.reduce(jnp.maximum, [r[1] for r in ranges])
        for where, copy in self.copies:
            @pl.when((where >= start) & (where < stop))
            def _():
                copy.start()
        self.kv[pl.ds(pl.multiple_of(stop * TOKENS, TOKENS), TOKENS), :] = jnp.zeros(
            (TOKENS, 2 * WIDTH), jnp.bfloat16
        )
        for where, copy in self.copies:
            @pl.when((where >= start) & (where < stop))
            def _():
                copy.wait()

    def segments(self, frames):
        found = jnp.zeros(frames.shape, jnp.int32)
        for end in self.ends:
            found = found + (frames >= end).astype(jnp.int32)
        return jnp.where(frames < 0, -1, found)

    def attend(self, which, q_ref, store):
        kv, scores, tops, totals, sums, low = (
            self.kv, self.scores, self.tops, self.totals, self.sums, self.low,
        )
        key_block, stop = self.keys_of(which)
        steps = lax.div(stop - key_block + 1, CHUNK // TOKENS)
        row_segment = self.segments(
            self.row_start + which * TOKENS + lax.broadcasted_iota(jnp.int32, (TOKENS, LANES), 0)
        )
        row_segment = jnp.concatenate([row_segment, row_segment], axis=1)
        queries = []
        for pair in range(PAIRS):
            one = q_ref[:, pair * LANES : (pair + 1) * LANES]
            zero = jnp.zeros_like(one)
            queries.append(
                jnp.concatenate([jnp.where(low, one, zero), jnp.where(low, zero, one)], axis=0)
            )
        tops[...] = jnp.full(tops.shape, masked_score, jnp.float32)
        totals[...] = jnp.zeros(totals.shape, jnp.float32)
        sums[...] = jnp.zeros(sums.shape, jnp.float32)

        def score(step, carry):
            start = pl.multiple_of(key_block * TOKENS + step * CHUNK, TOKENS)
            key_segment = self.segments(
                self.base + start + lax.broadcasted_iota(jnp.int32, (8, CHUNK), 1)
            )[:1]
            allowed = row_segment == key_segment
            allowed = jnp.concatenate([allowed, allowed], axis=0)
            for pair in range(PAIRS):
                keys = kv[pl.ds(start, CHUNK), pair * LANES : (pair + 1) * LANES]
                found = lax.dot_general(
                    queries[pair], keys, (((1,), (1,)), ((), ())),
                    preferred_element_type=jnp.float32,
                )
                found = jnp.where(allowed, found, masked_score)
                scores[step, pair] = found
                tops[pair] = jnp.maximum(
                    tops[pair], jnp.maximum(found[:, :LANES], found[:, LANES:])
                )
            return carry

        lax.fori_loop(0, steps, score, 0)
        for pair in range(PAIRS):
            top = jnp.max(tops[pair], axis=1, keepdims=True)
            tops[pair] = jnp.broadcast_to(top, (2 * TOKENS, LANES))

        def mix(step, carry):
            start = pl.multiple_of(key_block * TOKENS + step * CHUNK, TOKENS)
            for pair in range(PAIRS):
                found = scores[step, pair]
                left = jnp.exp(found[:, :LANES] - tops[pair])
                right = jnp.exp(found[:, LANES:] - tops[pair])
                totals[pair] = totals[pair] + (left + right)
                weights = jnp.concatenate([left, right], axis=1).astype(jnp.bfloat16)
                values = kv[
                    pl.ds(start, CHUNK), WIDTH + pair * LANES : WIDTH + (pair + 1) * LANES
                ]
                sums[pair] = sums[pair] + jnp.dot(
                    weights, values, preferred_element_type=jnp.float32
                )
            return carry

        lax.fori_loop(0, steps, mix, 0)
        for pair in range(PAIRS):
            row_total = jnp.sum(totals[pair], axis=1, keepdims=True)
            mixed = sums[pair] / row_total
            store(
                pair * LANES,
                jnp.where(low, mixed[:TOKENS], mixed[TOKENS:]).astype(jnp.bfloat16),
            )


def project(mixed, weights_ref, store):
    for tile in range(0, 16, 2):
        high, place = divmod(tile, 8)
        both = jnp.concatenate(
            [weights_ref[2 * place + high], weights_ref[2 * (place + 1) + high]], axis=1
        )
        store(tile * LANES, jnp.dot(mixed, both, preferred_element_type=jnp.float32))


HALF = D // 2
PAIR = 2 * LANES


def far_kernel(lengths_ref, place_ref, weights_hbm, q_ref, *rest):
    sources, (one_ref, two_ref), scratch = rest[:8], rest[8:10], rest[10:]
    weights, mixed, weight_sem = scratch[6:]
    fetch = pltpu.make_async_copy(weights_hbm, weights, weight_sem)
    fetch.start()
    attention = Attention(lengths_ref, place_ref, sources, *scratch[:6])
    which = lax.rem(attention.y + 2, 4)
    attention.load([which])

    def keep(start, value):
        mixed[:, start : start + LANES] = value

    attention.attend(which, q_ref, keep)
    fetch.wait()

    def store(start, value):
        out_ref = one_ref if start < HALF else two_ref
        start = start % HALF
        out_ref[:, start : start + PAIR] = value.astype(jnp.bfloat16)

    project(mixed[...], weights, store)


def near_kernel(lengths_ref, place_ref, q_ref, q3_ref, *rest):
    sources, out_ref, scratch = rest[:8], rest[8], rest[9:]
    attention = Attention(lengths_ref, place_ref, sources, *scratch)
    blocks = [lax.rem(attention.y + 1, 4), lax.rem(attention.y + 3, 4)]
    attention.load(blocks)
    for i, ref in enumerate((q_ref, q3_ref)):
        def keep(start, value):
            out_ref[i * TOKENS : (i + 1) * TOKENS, start : start + LANES] = value

        attention.attend(blocks[i], ref, keep)


def pass_kernel(mixed_ref, weights_ref, one_ref, two_ref, up_ref, down_ref):
    def store(start, value):
        up, down = value[:TOKENS], value[TOKENS:]
        span = slice(start, start + PAIR)
        if start < HALF:
            up = up + one_ref[:, span].astype(jnp.float32)
        else:
            down = down + two_ref[:, start - HALF : start - HALF + PAIR].astype(jnp.float32)
        up_ref[:, span] = up.astype(jnp.bfloat16)
        down_ref[:, span] = down.astype(jnp.bfloat16)

    project(mixed_ref[...], weights_ref, store)


def own_kernel(lengths_ref, place_ref, weights_hbm, q_ref, *rest):
    sources, out_ref, scratch = rest[:8], rest[8], rest[9:]
    weights, mixed, weight_sem = scratch[6:]
    fetch = pltpu.make_async_copy(weights_hbm, weights, weight_sem)
    fetch.start()
    attention = Attention(lengths_ref, place_ref, sources, *scratch[:6])
    attention.load([attention.y])

    def keep(start, value):
        mixed[:, start : start + LANES] = value

    attention.attend(attention.y, q_ref, keep)
    fetch.wait()

    def store(start, value):
        out_ref[:, start : start + PAIR] = value

    project(mixed[...], weights, store)


def finish_kernel(own_ref, up_ref, down_ref, resid_ref, earlier_ref, out_ref):
    branch = own_ref[...] + up_ref[...].astype(jnp.float32)
    branch = branch + down_ref[...].astype(jnp.float32)
    summed = resid_ref[...].astype(jnp.float32) + branch * (1.0 / math.sqrt(D))
    centered = summed - jnp.mean(summed, axis=1, keepdims=True)
    spread = jnp.mean(centered * centered, axis=1, keepdims=True)
    normed = centered * lax.rsqrt(spread + norm_epsilon)
    out_ref[...] = (earlier_ref[...] + normed) * (1.0 / TOP_K)


vmem = pl.BlockSpec(memory_space=pltpu.VMEM)
smem = pl.BlockSpec(memory_space=pltpu.SMEM)
anywhere = pl.BlockSpec(memory_space=pl.ANY)
attend_scratch = [
    pltpu.VMEM((13 * TOKENS, 2 * WIDTH), jnp.bfloat16),
    pltpu.VMEM((6, PAIRS, 2 * TOKENS, CHUNK), jnp.float32),
    pltpu.VMEM((PAIRS, 2 * TOKENS, LANES), jnp.float32),
    pltpu.VMEM((PAIRS, 2 * TOKENS, LANES), jnp.float32),
    pltpu.VMEM((PAIRS, 2 * TOKENS, LANES), jnp.float32),
    pltpu.SemaphoreType.DMA((12,)),
]
project_scratch = [
    pltpu.VMEM((16, ROW, LANES), jnp.bfloat16),
    pltpu.VMEM((TOKENS, WIDTH), jnp.bfloat16),
    pltpu.SemaphoreType.DMA,
]


def cost(flops, moved, exps=0):
    return pl.CostEstimate(flops=flops, bytes_accessed=moved, transcendentals=exps)


def array(*shape, dtype=jnp.bfloat16):
    return jax.ShapeDtypeStruct(shape, dtype)


def shift(value, amount, axis="y", size=4):
    return lax.ppermute(value, axis, [(i, (i + amount) % size) for i in range(size)])


def block(qkv, resid, earlier, lengths, teacher_out, student_out):
    teacher_new = (
        ema_decay * teacher_out.astype(jnp.float32)
        + (1.0 - ema_decay) * student_out.astype(jnp.float32)
    ).astype(jnp.bfloat16)
    place = jnp.stack([lax.axis_index("z"), lax.axis_index("y")]).astype(jnp.int32)

    packed = pl.pallas_call(
        pack_kernel,
        grid=(TOKENS // PACKED,),
        out_shape=(array(TOKENS, 2 * WIDTH),) * 4 + (array(TOKENS, WIDTH),) * 4,
        in_specs=[smem, pl.BlockSpec((PACKED, 3 * D), lambda i: (i, 0))],
        out_specs=(pl.BlockSpec((PACKED, 2 * WIDTH), lambda i: (i, 0)),) * 4
        + (pl.BlockSpec((PACKED, WIDTH), lambda i: (i, 0)),) * 4,
        cost_estimate=cost(0, 3 << 20),
        name="pack",
    )(place, qkv[0])
    kv, q = packed[:4], packed[4:]

    ring = 2 * lax.axis_size("z")
    kv_far = shift(kv[2], -2)
    kv_next = shift(kv[1], -1)
    kv_last = shift(kv[3], -3)
    own_after = shift(kv[0], -1, ("h", "z"), ring)
    own_before = shift(kv[0], 1, ("h", "z"), ring)
    others = jnp.concatenate([kv_next, kv_far, kv_last], axis=0)
    after = shift(others, -1, ("h", "z"), ring)
    before = shift(others, 1, ("h", "z"), ring)
    q_far = shift(q[2], -2)
    q_next = shift(q[1], -1)
    q_last = shift(q[3], -3)

    ring_weights = lax.all_to_all(
        jnp.broadcast_to(teacher_new[None], (16,) + teacher_new.shape), ("h", "z"), 0, 0, tiled=True
    )
    weights = lax.all_to_all(
        jnp.broadcast_to(ring_weights[None], (8,) + ring_weights.shape), ("x", "c"), 0, 0, tiled=True
    )
    weights = weights.reshape(16, ROW, LANES)

    sources = (kv[0], kv_next, kv_far, kv_last, own_before, before, own_after, after)
    places = [anywhere] * 8
    one, two = pl.pallas_call(
        far_kernel,
        out_shape=(array(TOKENS, HALF),) * 2,
        in_specs=[smem, smem, anywhere, vmem] + places,
        out_specs=(vmem,) * 2,
        scratch_shapes=attend_scratch + project_scratch,
        cost_estimate=cost(1 << 29, 4 << 20, 1 << 20),
        name="far",
    )(lengths, place, weights, q_far, *sources)
    one = shift(one, 1)
    two = shift(two, -1)
    mixed = pl.pallas_call(
        near_kernel,
        out_shape=array(2 * TOKENS, WIDTH),
        in_specs=[smem, smem, vmem, vmem] + places,
        out_specs=vmem,
        scratch_shapes=attend_scratch,
        cost_estimate=cost(1 << 30, 4 << 20, 2 << 20),
        name="near",
    )(lengths, place, q_next, q_last, *sources)
    up, down = pl.pallas_call(
        pass_kernel,
        out_shape=(array(TOKENS, D),) * 2,
        in_specs=[vmem] * 4,
        out_specs=(vmem,) * 2,
        cost_estimate=cost(4 * TOKENS * WIDTH * D, 4 << 20),
        name="pass",
    )(mixed, weights, one, two)
    up = shift(up, 1)
    down = shift(down, -1)
    own = pl.pallas_call(
        own_kernel,
        out_shape=array(TOKENS, D, dtype=jnp.float32),
        in_specs=[smem, smem, anywhere, vmem] + places,
        out_specs=vmem,
        scratch_shapes=attend_scratch + project_scratch,
        cost_estimate=cost(1 << 29, 4 << 20, 1 << 20),
        name="own",
    )(lengths, place, weights, q[0], *sources)
    rows = pl.BlockSpec((32, D), lambda i: (i, 0))
    targets = pl.pallas_call(
        finish_kernel,
        grid=(4,),
        out_shape=array(TOKENS, D, dtype=jnp.float32),
        in_specs=[rows] * 5,
        out_specs=rows,
        cost_estimate=cost(1 << 22, 5 << 20),
        name="finish",
    )(own, up, down, resid[0], earlier[0])
    return (targets[None], teacher_new)


def solution(mesh):
    fine = Mesh(
        mesh.devices.reshape(2, 4, 2, 8, 4), ("h", "x", "c", "z", "y")
    )
    packs, frames = ("h", "x", "c"), ("z", "y")
    placed = (
        P(packs, frames, None),
        P(packs, frames, None),
        P(packs, frames, None),
        P(packs, None),
        P(frames, packs),
        P(frames, packs),
    )
    return jax.shard_map(
        block,
        mesh=fine,
        in_specs=placed,
        out_specs=(P(packs, frames, None), P(frames, packs)),
        check_vma=False,
    )
```

```python
import functools
import math

import jax
import jax.numpy as jnp
from jax import lax
from jax.experimental import pallas as pl
from jax.experimental.pallas import tpu as pltpu
from jax.sharding import Mesh, PartitionSpec as P

D = 2048
HEAD_DIM = 64
TOP_K = 8
UTTS = 12
LANES = 128
TOKENS = 128
ROW = 512
WIDTH = 512
CHUNK = 256
PAIRS = WIDTH // LANES
PACKED = 32

ema_decay = 0.9
norm_epsilon = 1e-05
masked_score = -1e30


def pack_kernel(place_ref, qkv_ref, *outs):
    y = place_ref[1]
    low = lax.broadcasted_iota(jnp.int32, (PACKED, LANES), 1) < HEAD_DIM
    for turn in range(4):
        target = lax.rem(y + 4 - turn, 4)
        odd = lax.rem(target, 2) == 1
        half = lax.div(target, 2) * LANES
        for part in range(3):
            for pair in range(PAIRS):
                base = part * D + pair * 512
                first = qkv_ref[:, pl.ds(pl.multiple_of(base + half, LANES), LANES)].astype(jnp.float32)
                second = qkv_ref[:, pl.ds(pl.multiple_of(base + 256 + half, LANES), LANES)].astype(jnp.float32)
                left = jnp.where(odd, pltpu.roll(first, HEAD_DIM, 1), first)
                right = jnp.where(odd, second, pltpu.roll(second, HEAD_DIM, 1))
                both = jnp.where(low, left, right)
                if part == 0:
                    both = both * (1.0 / math.sqrt(HEAD_DIM))
                start = part * WIDTH + pair * LANES
                outs[turn][:, start : start + LANES] = both.astype(jnp.bfloat16)


class Attention:
    def __init__(self, lengths_ref, place_ref, sources, kv, scores, tops, totals, sums, sems):
        self.kv, self.scores, self.tops, self.totals, self.sums = kv, scores, tops, totals, sums
        self.row_start = place_ref[0] * ROW
        self.y = place_ref[1]
        self.base = self.row_start - ROW
        self.ends = []
        total = jnp.int32(0)
        for j in range(UTTS):
            total = total + lengths_ref[0, j]
            self.ends.append(total)
        self.low = lax.broadcasted_iota(jnp.int32, (TOKENS, LANES), 1) < HEAD_DIM
        pieces, before, after = sources
        self.copies = []
        for turn in range(4):
            slot = lax.rem(self.y + turn, 4)
            span = pl.ds(turn * TOKENS, TOKENS)
            views = (before.at[span], pieces[turn].at[:, pl.ds(WIDTH, 2 * WIDTH)], after.at[span])
            for row, view in enumerate(views):
                where = slot + 4 * row
                target = kv.at[pl.ds(pl.multiple_of(where * TOKENS, TOKENS), TOKENS)]
                copy = pltpu.make_async_copy(view, target, sems.at[3 * turn + row])
                self.copies.append((where, copy))

    def keys_of(self, which):
        first = self.row_start + which * TOKENS
        last = first + TOKENS - 1
        begin = jnp.int32(0)
        finish = jnp.int32(0)
        for end in reversed(self.ends):
            finish = jnp.where(end > last, end, finish)
        for end in self.ends:
            begin = jnp.where(end <= first, end, begin)
        start = lax.div(begin - self.base, TOKENS)
        stop = lax.div(finish - self.base + TOKENS - 1, TOKENS)
        return start, stop

    def load(self, blocks):
        ranges = [self.keys_of(which) for which in blocks]
        start = functools.reduce(jnp.minimum, [r[0] for r in ranges])
        stop = functools.reduce(jnp.maximum, [r[1] for r in ranges])
        for where, copy in self.copies:
            @pl.when((where >= start) & (where < stop))
            def _():
                copy.start()
        self.kv[pl.ds(pl.multiple_of(stop * TOKENS, TOKENS), TOKENS), :] = jnp.zeros(
            (TOKENS, 2 * WIDTH), jnp.bfloat16
        )
        for where, copy in self.copies:
            @pl.when((where >= start) & (where < stop))
            def _():
                copy.wait()

    def segments(self, frames):
        found = jnp.zeros(frames.shape, jnp.int32)
        for end in self.ends:
            found = found + (frames >= end).astype(jnp.int32)
        return jnp.where(frames < 0, -1, found)

    def attend(self, which, q_ref, store):
        kv, scores, tops, totals, sums, low = (
            self.kv, self.scores, self.tops, self.totals, self.sums, self.low,
        )
        key_block, stop = self.keys_of(which)
        steps = lax.div(stop - key_block + 1, CHUNK // TOKENS)
        row_segment = self.segments(
            self.row_start + which * TOKENS + lax.broadcasted_iota(jnp.int32, (TOKENS, LANES), 0)
        )
        row_segment = jnp.concatenate([row_segment, row_segment], axis=1)
        queries = []
        for pair in range(PAIRS):
            one = q_ref[:, pair * LANES : (pair + 1) * LANES]
            zero = jnp.zeros_like(one)
            queries.append(
                jnp.concatenate([jnp.where(low, one, zero), jnp.where(low, zero, one)], axis=0)
            )
        tops[...] = jnp.full(tops.shape, masked_score, jnp.float32)
        totals[...] = jnp.zeros(totals.shape, jnp.float32)
        sums[...] = jnp.zeros(sums.shape, jnp.float32)

        def score(step, carry):
            start = pl.multiple_of(key_block * TOKENS + step * CHUNK, TOKENS)
            key_segment = self.segments(
                self.base + start + lax.broadcasted_iota(jnp.int32, (8, CHUNK), 1)
            )[:1]
            allowed = row_segment == key_segment
            allowed = jnp.concatenate([allowed, allowed], axis=0)
            for pair in range(PAIRS):
                keys = kv[pl.ds(start, CHUNK), pair * LANES : (pair + 1) * LANES]
                found = lax.dot_general(
                    queries[pair], keys, (((1,), (1,)), ((), ())),
                    preferred_element_type=jnp.float32,
                )
                found = jnp.where(allowed, found, masked_score)
                scores[step, pair] = found
                tops[pair] = jnp.maximum(
                    tops[pair], jnp.maximum(found[:, :LANES], found[:, LANES:])
                )
            return carry

        lax.fori_loop(0, steps, score, 0)
        for pair in range(PAIRS):
            top = jnp.max(tops[pair], axis=1, keepdims=True)
            tops[pair] = jnp.broadcast_to(top, (2 * TOKENS, LANES))

        def mix(step, carry):
            start = pl.multiple_of(key_block * TOKENS + step * CHUNK, TOKENS)
            for pair in range(PAIRS):
                found = scores[step, pair]
                left = jnp.exp(found[:, :LANES] - tops[pair])
                right = jnp.exp(found[:, LANES:] - tops[pair])
                totals[pair] = totals[pair] + (left + right)
                weights = jnp.concatenate([left, right], axis=1).astype(jnp.bfloat16)
                values = kv[
                    pl.ds(start, CHUNK), WIDTH + pair * LANES : WIDTH + (pair + 1) * LANES
                ]
                sums[pair] = sums[pair] + jnp.dot(
                    weights, values, preferred_element_type=jnp.float32
                )
            return carry

        lax.fori_loop(0, steps, mix, 0)
        for pair in range(PAIRS):
            row_total = jnp.sum(totals[pair], axis=1, keepdims=True)
            mixed = sums[pair] / row_total
            store(
                pair * LANES,
                jnp.where(low, mixed[:TOKENS], mixed[TOKENS:]).astype(jnp.bfloat16),
            )


def project(mixed, weights_ref, store):
    for tile in range(8):
        high, place = divmod(tile, 4)
        both = jnp.concatenate([weights_ref[0, place, high], weights_ref[1, place, high]], axis=1)
        store(tile * PAIR, jnp.dot(mixed, both, preferred_element_type=jnp.float32))


PAIR = 2 * LANES


def rows_kernel(
    offset, lengths_ref, place_ref, own_weights, other_weights, own, next_piece, far, last, before, after,
    out_ref, kv, scores, tops, totals, sums, weights, queries, mixed, sems,
):
    core = place_ref[2]
    fetches = [
        pltpu.make_async_copy(own_weights, weights.at[core], sems.at[12]),
        pltpu.make_async_copy(other_weights, weights.at[1 - core], sems.at[13]),
    ]
    pieces = (own, next_piece, far, last)
    attention = Attention(
        lengths_ref, place_ref, (pieces, before, after), kv, scores, tops, totals, sums, sems
    )
    which = lax.rem(attention.y + offset, 4)
    ask = pltpu.make_async_copy(pieces[offset].at[:, pl.ds(0, WIDTH)], queries, sems.at[14])
    ask.start()
    for fetch in fetches:
        fetch.start()
    attention.load([which])
    ask.wait()

    def keep(start, value):
        mixed[:, start : start + LANES] = value

    attention.attend(which, queries, keep)
    for fetch in fetches:
        fetch.wait()

    def store(start, value):
        out_ref[:, start : start + PAIR] = value.astype(out_ref.dtype)

    project(mixed[...], weights, store)


def finish_kernel(own_ref, one_ref, two_ref, three_ref, resid_ref, earlier_ref, out_ref):
    branch = own_ref[...] + one_ref[...].astype(jnp.float32)
    branch = branch + two_ref[...].astype(jnp.float32)
    branch = branch + three_ref[...].astype(jnp.float32)
    summed = resid_ref[...].astype(jnp.float32) + branch * (1.0 / math.sqrt(D))
    centered = summed - jnp.mean(summed, axis=1, keepdims=True)
    spread = jnp.mean(centered * centered, axis=1, keepdims=True)
    normed = centered * lax.rsqrt(spread + norm_epsilon)
    out_ref[...] = (earlier_ref[...] + normed) * (1.0 / TOP_K)


vmem = pl.BlockSpec(memory_space=pltpu.VMEM)
smem = pl.BlockSpec(memory_space=pltpu.SMEM)
anywhere = pl.BlockSpec(memory_space=pl.ANY)
scratch = [
    pltpu.VMEM((13 * TOKENS, 2 * WIDTH), jnp.bfloat16),
    pltpu.VMEM((6, PAIRS, 2 * TOKENS, CHUNK), jnp.float32),
    pltpu.VMEM((PAIRS, 2 * TOKENS, LANES), jnp.float32),
    pltpu.VMEM((PAIRS, 2 * TOKENS, LANES), jnp.float32),
    pltpu.VMEM((PAIRS, 2 * TOKENS, LANES), jnp.float32),
    pltpu.VMEM((2, 4, 2, ROW, LANES), jnp.bfloat16),
    pltpu.VMEM((TOKENS, WIDTH), jnp.bfloat16),
    pltpu.VMEM((TOKENS, WIDTH), jnp.bfloat16),
    pltpu.SemaphoreType.DMA((15,)),
]


def cost(flops, moved, exps=0):
    return pl.CostEstimate(flops=flops, bytes_accessed=moved, transcendentals=exps)


def limit(mebibytes):
    return pltpu.CompilerParams(vmem_limit_bytes=mebibytes << 20)


def array(*shape, dtype=jnp.bfloat16):
    return jax.ShapeDtypeStruct(shape, dtype)


def shift(value, amount, axis="y", size=4):
    return lax.ppermute(value, axis, [(i, (i + amount) % size) for i in range(size)])


def block(qkv, resid, earlier, lengths, teacher_out, student_out):
    teacher_new = (
        ema_decay * teacher_out.astype(jnp.float32)
        + (1.0 - ema_decay) * student_out.astype(jnp.float32)
    ).astype(jnp.bfloat16)
    place = jnp.stack([lax.axis_index(name) for name in ("z", "y", "c")]).astype(jnp.int32)

    packed = pl.pallas_call(
        pack_kernel,
        grid=(TOKENS // PACKED,),
        out_shape=(array(TOKENS, 3 * WIDTH),) * 4,
        in_specs=[smem, pl.BlockSpec((PACKED, 3 * D), lambda i: (i, 0))],
        out_specs=(pl.BlockSpec((PACKED, 3 * WIDTH), lambda i: (i, 0)),) * 4,
        compiler_params=limit(12),
        cost_estimate=cost(0, 3 << 20),
        name="pack",
    )(place, qkv[0])

    pieces = [packed[0]]
    for turn in (1, 2, 3):
        pieces.append(shift(packed[turn], -turn))
    ring = 2 * lax.axis_size("z")
    keys = jnp.concatenate([piece[:, WIDTH:] for piece in pieces], axis=0)
    after = shift(keys, -1, ("h", "z"), ring)
    before = shift(keys, 1, ("h", "z"), ring)

    ring_weights = lax.all_to_all(
        jnp.broadcast_to(teacher_new[None], (16,) + teacher_new.shape), ("h", "z"), 0, 0, tiled=True
    )
    ring_weights = ring_weights.reshape(2, ROW, LANES)
    own_weights = lax.all_to_all(
        jnp.broadcast_to(ring_weights[None], (4,) + ring_weights.shape), "x", 0, 0, tiled=True
    )
    other_weights = shift(own_weights, 1, "c", 2)

    def rows_of(offset, dtype):
        return pl.pallas_call(
            functools.partial(rows_kernel, offset),
            out_shape=array(TOKENS, D, dtype=dtype),
            in_specs=[smem, smem] + [anywhere] * 8,
            out_specs=vmem,
            scratch_shapes=scratch,
            compiler_params=limit(24),
            cost_estimate=cost(1 << 29, 4 << 20, 1 << 20),
            name="rows",
        )(lengths, place, own_weights, other_weights, *pieces, before, after)

    arrived = []
    for offset in (2, 1, 3):
        part = rows_of(offset, jnp.bfloat16)
        arrived.append(shift(part, offset))
    own = rows_of(0, jnp.float32)
    rows = pl.BlockSpec((32, D), lambda i: (i, 0))
    targets = pl.pallas_call(
        finish_kernel,
        grid=(4,),
        out_shape=array(TOKENS, D, dtype=jnp.float32),
        in_specs=[rows] * 6,
        out_specs=rows,
        compiler_params=limit(12),
        cost_estimate=cost(1 << 22, 5 << 20),
        name="finish",
    )(own, *arrived, resid[0], earlier[0])
    return (targets[None], teacher_new)


def solution(mesh):
    fine = Mesh(
        mesh.devices.reshape(2, 4, 2, 8, 4), ("h", "x", "c", "z", "y")
    )
    packs, frames = ("h", "x", "c"), ("z", "y")
    placed = (
        P(packs, frames, None),
        P(packs, frames, None),
        P(packs, frames, None),
        P(packs, None),
        P(frames, packs),
        P(frames, packs),
    )
    return jax.shard_map(
        block,
        mesh=fine,
        in_specs=placed,
        out_specs=(P(packs, frames, None), P(frames, packs)),
        check_vma=False,
    )
```

```python
import functools
import math

import jax
import jax.numpy as jnp
from jax import lax
from jax.experimental import pallas as pl
from jax.experimental.pallas import tpu as pltpu
from jax.sharding import Mesh, PartitionSpec as P

D = 2048
HEAD_DIM = 64
TOP_K = 8
UTTS = 12
LANES = 128
TOKENS = 128
ROW = 512
WIDTH = 512
CHUNK = 256
PAIRS = WIDTH // LANES
PACKED = 32

ema_decay = 0.9
norm_epsilon = 1e-05
masked_score = -1e30


def pack_kernel(place_ref, qkv_ref, *outs):
    y = place_ref[1]
    low = lax.broadcasted_iota(jnp.int32, (PACKED, LANES), 1) < HEAD_DIM
    for turn in range(4):
        target = lax.rem(y + 4 - turn, 4)
        odd = lax.rem(target, 2) == 1
        half = lax.div(target, 2) * LANES
        for part in range(3):
            for pair in range(PAIRS):
                base = part * D + pair * 512
                first = qkv_ref[:, pl.ds(pl.multiple_of(base + half, LANES), LANES)].astype(jnp.float32)
                second = qkv_ref[:, pl.ds(pl.multiple_of(base + 256 + half, LANES), LANES)].astype(jnp.float32)
                left = jnp.where(odd, pltpu.roll(first, HEAD_DIM, 1), first)
                right = jnp.where(odd, second, pltpu.roll(second, HEAD_DIM, 1))
                both = jnp.where(low, left, right)
                if part == 0:
                    both = both * (1.0 / math.sqrt(HEAD_DIM))
                start = part * WIDTH + pair * LANES
                outs[turn][:, start : start + LANES] = both.astype(jnp.bfloat16)


class Attention:
    def __init__(self, lengths_ref, place_ref):
        self.row_start = place_ref[0] * ROW
        self.y = place_ref[1]
        self.base = self.row_start - ROW
        self.ends = []
        total = jnp.int32(0)
        for j in range(UTTS):
            total = total + lengths_ref[0, j]
            self.ends.append(total)
        self.low = lax.broadcasted_iota(jnp.int32, (TOKENS, LANES), 1) < HEAD_DIM

    def steps_of(self, which):
        first = self.row_start + which * TOKENS
        last = first + TOKENS - 1
        begin = jnp.int32(0)
        finish = jnp.int32(0)
        for end in reversed(self.ends):
            finish = jnp.where(end > last, end, finish)
        for end in self.ends:
            begin = jnp.where(end <= first, end, begin)
        return lax.div(begin - self.base, CHUNK), lax.div(finish - self.base + CHUNK - 1, CHUNK)

    def segments(self, frames):
        found = jnp.zeros(frames.shape, jnp.int32)
        for end in self.ends:
            found = found + (frames >= end).astype(jnp.int32)
        return jnp.where(frames < 0, -1, found)

    def attend(self, which, queries, kv, step_of, count, scores, state, prior=None, ready=None):
        low = self.low
        tops, totals, sums = (state.at[i] for i in range(3))
        row_segment = self.segments(
            self.row_start + which * TOKENS + lax.broadcasted_iota(jnp.int32, (TOKENS, LANES), 0)
        )
        row_segment = jnp.concatenate([row_segment, row_segment], axis=1)
        stacked = []
        for pair in range(PAIRS):
            one = queries[:, pair * LANES : (pair + 1) * LANES]
            zero = jnp.zeros_like(one)
            stacked.append(
                jnp.concatenate([jnp.where(low, one, zero), jnp.where(low, zero, one)], axis=0)
            )
        tops[...] = jnp.full(tops.shape, masked_score, jnp.float32)

        def score(turn, carry):
            step, place = step_of(turn)
            start = pl.multiple_of(place * CHUNK, CHUNK)
            key_segment = self.segments(
                self.base + step * CHUNK + lax.broadcasted_iota(jnp.int32, (8, CHUNK), 1)
            )[:1]
            allowed = row_segment == key_segment
            allowed = jnp.concatenate([allowed, allowed], axis=0)
            for pair in range(PAIRS):
                keys = kv[pl.ds(start, CHUNK), pair * LANES : (pair + 1) * LANES]
                found = lax.dot_general(
                    stacked[pair], keys, (((1,), (1,)), ((), ())),
                    preferred_element_type=jnp.float32,
                )
                found = jnp.where(allowed, found, masked_score)
                scores[turn, pair] = found
                tops[pair] = jnp.maximum(
                    tops[pair], jnp.maximum(found[:, :LANES], found[:, LANES:])
                )
            return carry

        lax.fori_loop(0, count, score, 0)
        if ready is not None:
            ready()
        for pair in range(PAIRS):
            top = jnp.max(tops[pair], axis=1, keepdims=True)
            top = jnp.broadcast_to(top, (2 * TOKENS, LANES))
            if prior is None:
                tops[pair] = top
                totals[pair] = jnp.zeros((2 * TOKENS, LANES), jnp.float32)
                sums[pair] = jnp.zeros((2 * TOKENS, LANES), jnp.float32)
            else:
                top = jnp.maximum(top, prior[0, pair])
                tops[pair] = top
                factor = jnp.exp(prior[0, pair] - top)
                totals[pair] = prior[1, pair] * factor
                sums[pair] = prior[2, pair] * factor

        def mix(turn, carry):
            _, place = step_of(turn)
            start = pl.multiple_of(place * CHUNK, CHUNK)
            for pair in range(PAIRS):
                found = scores[turn, pair]
                left = jnp.exp(found[:, :LANES] - tops[pair])
                right = jnp.exp(found[:, LANES:] - tops[pair])
                totals[pair] = totals[pair] + (left + right)
                weights = jnp.concatenate([left, right], axis=1).astype(jnp.bfloat16)
                values = kv[
                    pl.ds(start, CHUNK), WIDTH + pair * LANES : WIDTH + (pair + 1) * LANES
                ]
                sums[pair] = sums[pair] + jnp.dot(
                    weights, values, preferred_element_type=jnp.float32
                )
            return carry

        lax.fori_loop(0, count, mix, 0)


def local_kernel(lengths_ref, place_ref, own, next_piece, far, last, *rest):
    outs, (kv, queries, scores, states, sems) = rest[:4], rest[4:]
    attention = Attention(lengths_ref, place_ref)
    pieces = (own, next_piece, far, last)
    asks, copies = [], []
    for turn in range(4):
        slot = lax.rem(attention.y + turn, 4)
        asks.append(
            pltpu.make_async_copy(
                pieces[turn].at[:, pl.ds(0, WIDTH)], queries.at[turn], sems.at[4 + turn]
            )
        )
        copies.append(
            pltpu.make_async_copy(
                pieces[turn].at[:, pl.ds(WIDTH, 2 * WIDTH)],
                kv.at[pl.ds(pl.multiple_of(slot * TOKENS, TOKENS), TOKENS)],
                sems.at[turn],
            )
        )
    for copy in asks + copies:
        copy.start()
    for copy in asks + copies:
        copy.wait()
    stores = []
    for i, offset in enumerate((2, 1, 3, 0)):
        if i >= 2:
            stores[i - 2].wait()
        which = lax.rem(attention.y + offset, 4)
        start, stop = attention.steps_of(which)
        start, stop = jnp.maximum(start, 2), jnp.minimum(stop, 4)
        attention.attend(
            which, queries[offset], kv,
            lambda turn: (start + turn, start + turn - 2), stop - start,
            scores, states.at[i % 2],
        )
        stores.append(pltpu.make_async_copy(states.at[i % 2], outs[offset], sems.at[8 + i]))
        stores[i].start()
    stores[2].wait()
    stores[3].wait()


def project(mixed, weights_ref, store):
    for tile in range(8):
        high, place = divmod(tile, 4)
        both = jnp.concatenate([weights_ref[0, place, high], weights_ref[1, place, high]], axis=1)
        store(tile * PAIR, jnp.dot(mixed, both, preferred_element_type=jnp.float32))


PAIR = 2 * LANES


def rows_kernel(
    offset, lengths_ref, place_ref, own_weights, other_weights, queries,
    own_before, rest_before, own_after, rest_after, prior_hbm, out_ref,
    kv, asked, prior, scores, state, weights, mixed, sems,
):
    core = place_ref[2]
    fetches = [
        pltpu.make_async_copy(own_weights, weights.at[core], sems.at[8]),
        pltpu.make_async_copy(other_weights, weights.at[1 - core], sems.at[9]),
    ]
    attention = Attention(lengths_ref, place_ref)
    which = lax.rem(attention.y + offset, 4)
    start, stop = attention.steps_of(which)
    ahead = jnp.maximum(2 - start, 0)
    behind = jnp.maximum(stop - 4, 0)
    copies = []
    for side, (first, others) in enumerate(((own_before, rest_before), (own_after, rest_after))):
        for turn in range(4):
            slot = lax.rem(attention.y + turn, 4)
            half = lax.div(slot, 2)
            copy = pltpu.make_async_copy(
                others.at[pl.ds((turn - 1) * TOKENS, TOKENS)] if turn else first,
                kv.at[pl.ds(pl.multiple_of((4 * side + slot) * TOKENS, TOKENS), TOKENS)],
                sems.at[4 * side + turn],
            )
            copies.append((half < behind if side else half >= 2 - ahead, copy))
    ask = pltpu.make_async_copy(queries.at[:, pl.ds(0, WIDTH)], asked, sems.at[10])
    recall = pltpu.make_async_copy(prior_hbm, prior, sems.at[11])
    ask.start()
    for wanted, copy in copies:
        @pl.when(wanted)
        def _():
            copy.start()
    recall.start()
    for fetch in fetches:
        fetch.start()
    ask.wait()
    for wanted, copy in copies:
        @pl.when(wanted)
        def _():
            copy.wait()

    def step_of(turn):
        early = turn < ahead
        step = jnp.where(early, 2 - ahead + turn, 4 + turn - ahead)
        return step, jnp.where(early, step, step - 2)

    attention.attend(
        which, asked[...], kv, step_of, ahead + behind, scores, state, prior, recall.wait
    )
    for pair in range(PAIRS):
        row_total = jnp.sum(state[1, pair], axis=1, keepdims=True)
        found = state[2, pair] / row_total
        mixed[:, pair * LANES : (pair + 1) * LANES] = jnp.where(
            attention.low, found[:TOKENS], found[TOKENS:]
        ).astype(jnp.bfloat16)
    for fetch in fetches:
        fetch.wait()

    def store(start, value):
        out_ref[:, start : start + PAIR] = value.astype(out_ref.dtype)

    project(mixed[...], weights, store)


def finish_kernel(own_ref, one_ref, two_ref, three_ref, resid_ref, earlier_ref, out_ref):
    branch = own_ref[...] + one_ref[...].astype(jnp.float32)
    branch = branch + two_ref[...].astype(jnp.float32)
    branch = branch + three_ref[...].astype(jnp.float32)
    summed = resid_ref[...].astype(jnp.float32) + branch * (1.0 / math.sqrt(D))
    centered = summed - jnp.mean(summed, axis=1, keepdims=True)
    spread = jnp.mean(centered * centered, axis=1, keepdims=True)
    normed = centered * lax.rsqrt(spread + norm_epsilon)
    out_ref[...] = (earlier_ref[...] + normed) * (1.0 / TOP_K)


vmem = pl.BlockSpec(memory_space=pltpu.VMEM)
smem = pl.BlockSpec(memory_space=pltpu.SMEM)
anywhere = pl.BlockSpec(memory_space=pl.ANY)
hbm = pl.BlockSpec(memory_space=pltpu.HBM)
running = (3, PAIRS, 2 * TOKENS, LANES)
local_scratch = [
    pltpu.VMEM((ROW, 2 * WIDTH), jnp.bfloat16),
    pltpu.VMEM((4, TOKENS, WIDTH), jnp.bfloat16),
    pltpu.VMEM((2, PAIRS, 2 * TOKENS, CHUNK), jnp.float32),
    pltpu.VMEM((2,) + running, jnp.float32),
    pltpu.SemaphoreType.DMA((12,)),
]
rows_scratch = [
    pltpu.VMEM((2 * ROW, 2 * WIDTH), jnp.bfloat16),
    pltpu.VMEM((TOKENS, WIDTH), jnp.bfloat16),
    pltpu.VMEM(running, jnp.float32),
    pltpu.VMEM((4, PAIRS, 2 * TOKENS, CHUNK), jnp.float32),
    pltpu.VMEM(running, jnp.float32),
    pltpu.VMEM((2, 4, 2, ROW, LANES), jnp.bfloat16),
    pltpu.VMEM((TOKENS, WIDTH), jnp.bfloat16),
    pltpu.SemaphoreType.DMA((12,)),
]


def cost(flops, moved, exps=0):
    return pl.CostEstimate(flops=flops, bytes_accessed=moved, transcendentals=exps)


def limit(mebibytes):
    return pltpu.CompilerParams(vmem_limit_bytes=mebibytes << 20)


def array(*shape, dtype=jnp.bfloat16):
    return jax.ShapeDtypeStruct(shape, dtype)


def shift(value, amount, axis="y", size=4):
    return lax.ppermute(value, axis, [(i, (i + amount) % size) for i in range(size)])


def block(qkv, resid, earlier, lengths, teacher_out, student_out):
    teacher_new = (
        ema_decay * teacher_out.astype(jnp.float32)
        + (1.0 - ema_decay) * student_out.astype(jnp.float32)
    ).astype(jnp.bfloat16)
    place = jnp.stack([lax.axis_index(name) for name in ("z", "y", "c")]).astype(jnp.int32)

    packed = pl.pallas_call(
        pack_kernel,
        grid=(TOKENS // PACKED,),
        out_shape=(array(TOKENS, 3 * WIDTH),) * 4,
        in_specs=[smem, pl.BlockSpec((PACKED, 3 * D), lambda i: (i, 0))],
        out_specs=(pl.BlockSpec((PACKED, 3 * WIDTH), lambda i: (i, 0)),) * 4,
        compiler_params=limit(12),
        cost_estimate=cost(0, 3 << 20),
        name="pack",
    )(place, qkv[0])

    pieces = [packed[0]]
    for turn in (1, 2, 3):
        pieces.append(shift(packed[turn], -turn))
    ring = 2 * lax.axis_size("z")
    own_after = shift(packed[0][:, WIDTH:], -1, ("h", "z"), ring)
    own_before = shift(packed[0][:, WIDTH:], 1, ("h", "z"), ring)
    keys = jnp.concatenate([piece[:, WIDTH:] for piece in pieces[1:]], axis=0)
    rest_after = shift(keys, -1, ("h", "z"), ring)
    rest_before = shift(keys, 1, ("h", "z"), ring)

    ring_weights = lax.all_to_all(
        jnp.broadcast_to(teacher_new[None], (16,) + teacher_new.shape), ("h", "z"), 0, 0, tiled=True
    )
    ring_weights = ring_weights.reshape(2, ROW, LANES)
    own_weights = lax.all_to_all(
        jnp.broadcast_to(ring_weights[None], (4,) + ring_weights.shape), "x", 0, 0, tiled=True
    )
    other_weights = shift(own_weights, 1, "c", 2)

    local = pl.pallas_call(
        local_kernel,
        out_shape=(array(*running, dtype=jnp.float32),) * 4,
        in_specs=[smem, smem] + [hbm] * 4,
        out_specs=(hbm,) * 4,
        scratch_shapes=local_scratch,
        compiler_params=limit(16),
        cost_estimate=cost(1 << 30, 8 << 20, 2 << 20),
        name="local",
    )(lengths, place, *pieces)

    def rows_of(offset, dtype):
        return pl.pallas_call(
            functools.partial(rows_kernel, offset),
            out_shape=array(TOKENS, D, dtype=dtype),
            in_specs=[smem, smem] + [anywhere] * 2 + [hbm] + [anywhere] * 4 + [hbm],
            out_specs=vmem,
            scratch_shapes=rows_scratch,
            compiler_params=limit(20),
            cost_estimate=cost(1 << 29, 4 << 20, 1 << 20),
            name="rows",
        )(
            lengths, place, own_weights, other_weights, pieces[offset],
            own_before, rest_before, own_after, rest_after, local[offset],
        )

    arrived = []
    for offset in (2, 1, 3):
        part = rows_of(offset, jnp.bfloat16)
        arrived.append(shift(part, offset))
    own = rows_of(0, jnp.float32)
    rows = pl.BlockSpec((32, D), lambda i: (i, 0))
    targets = pl.pallas_call(
        finish_kernel,
        grid=(4,),
        out_shape=array(TOKENS, D, dtype=jnp.float32),
        in_specs=[rows] * 6,
        out_specs=rows,
        compiler_params=limit(12),
        cost_estimate=cost(1 << 22, 5 << 20),
        name="finish",
    )(own, *arrived, resid[0], earlier[0])
    return (targets[None], teacher_new)


def solution(mesh):
    fine = Mesh(
        mesh.devices.reshape(2, 4, 2, 8, 4), ("h", "x", "c", "z", "y")
    )
    packs, frames = ("h", "x", "c"), ("z", "y")
    placed = (
        P(packs, frames, None),
        P(packs, frames, None),
        P(packs, frames, None),
        P(packs, None),
        P(frames, packs),
        P(frames, packs),
    )
    return jax.shard_map(
        block,
        mesh=fine,
        in_specs=placed,
        out_specs=(P(packs, frames, None), P(frames, packs)),
        check_vma=False,
    )
```

```python
import functools
import math

import jax
import jax.numpy as jnp
from jax import lax
from jax.experimental import pallas as pl
from jax.experimental.pallas import tpu as pltpu
from jax.sharding import Mesh, PartitionSpec as P

D = 2048
HEAD_DIM = 64
TOP_K = 8
UTTS = 12
LANES = 128
TOKENS = 128
ROW = 512
WIDTH = 512
CHUNK = 256
PAIRS = WIDTH // LANES
PACKED = 32

ema_decay = 0.9
norm_epsilon = 1e-05
masked_score = -1e30


def pack_kernel(place_ref, qkv_ref, *outs):
    y = place_ref[1]
    low = lax.broadcasted_iota(jnp.int32, (PACKED, LANES), 1) < HEAD_DIM
    for turn in range(4):
        target = lax.rem(y + 4 - turn, 4)
        odd = lax.rem(target, 2) == 1
        half = lax.div(target, 2) * LANES
        for part in range(3):
            for pair in range(PAIRS):
                base = part * D + pair * 512
                first = qkv_ref[:, pl.ds(pl.multiple_of(base + half, LANES), LANES)].astype(jnp.float32)
                second = qkv_ref[:, pl.ds(pl.multiple_of(base + 256 + half, LANES), LANES)].astype(jnp.float32)
                left = jnp.where(odd, pltpu.roll(first, HEAD_DIM, 1), first)
                right = jnp.where(odd, second, pltpu.roll(second, HEAD_DIM, 1))
                both = jnp.where(low, left, right)
                if part == 0:
                    both = both * (1.0 / math.sqrt(HEAD_DIM))
                start = part * WIDTH + pair * LANES
                outs[turn][:, start : start + LANES] = both.astype(jnp.bfloat16)


class Attention:
    def __init__(self, lengths_ref, place_ref):
        self.row_start = place_ref[0] * ROW
        self.y = place_ref[1]
        self.base = self.row_start - ROW
        self.ends = []
        total = jnp.int32(0)
        for j in range(UTTS):
            total = total + lengths_ref[0, j]
            self.ends.append(total)
        self.low = lax.broadcasted_iota(jnp.int32, (TOKENS, LANES), 1) < HEAD_DIM

    def steps_of(self, which):
        first = self.row_start + which * TOKENS
        last = first + TOKENS - 1
        begin = jnp.int32(0)
        finish = jnp.int32(0)
        for end in reversed(self.ends):
            finish = jnp.where(end > last, end, finish)
        for end in self.ends:
            begin = jnp.where(end <= first, end, begin)
        return lax.div(begin - self.base, CHUNK), lax.div(finish - self.base + CHUNK - 1, CHUNK)

    def segments(self, frames):
        found = jnp.zeros(frames.shape, jnp.int32)
        for end in self.ends:
            found = found + (frames >= end).astype(jnp.int32)
        return jnp.where(frames < 0, -1, found)

    def attend(self, which, queries, kv, step_of, count, scores, state, prior=None, ready=None):
        low = self.low
        tops, totals, sums = (state.at[pl.ds(PAIRS * i, PAIRS)] for i in range(3))
        row_segment = self.segments(
            self.row_start + which * TOKENS + lax.broadcasted_iota(jnp.int32, (TOKENS, LANES), 0)
        )
        row_segment = jnp.concatenate([row_segment, row_segment], axis=1)
        stacked = []
        for pair in range(PAIRS):
            one = queries[pair]
            zero = jnp.zeros_like(one)
            stacked.append(
                jnp.concatenate([jnp.where(low, one, zero), jnp.where(low, zero, one)], axis=0)
            )
        tops[...] = jnp.full(tops.shape, masked_score, jnp.float32)

        def score(turn, carry):
            step, place = step_of(turn)
            start = pl.multiple_of(place * CHUNK, CHUNK)
            key_segment = self.segments(
                self.base + step * CHUNK + lax.broadcasted_iota(jnp.int32, (8, CHUNK), 1)
            )[:1]
            allowed = row_segment == key_segment
            allowed = jnp.concatenate([allowed, allowed], axis=0)
            for pair in range(PAIRS):
                keys = kv[pl.ds(start, CHUNK), pair * LANES : (pair + 1) * LANES]
                found = lax.dot_general(
                    stacked[pair], keys, (((1,), (1,)), ((), ())),
                    preferred_element_type=jnp.float32,
                )
                found = jnp.where(allowed, found, masked_score)
                scores[turn, pair] = found
                tops[pair] = jnp.maximum(
                    tops[pair], jnp.maximum(found[:, :LANES], found[:, LANES:])
                )
            return carry

        lax.fori_loop(0, count, score, 0)
        if ready is not None:
            ready()
        for pair in range(PAIRS):
            top = jnp.max(tops[pair], axis=1, keepdims=True)
            top = jnp.broadcast_to(top, (2 * TOKENS, LANES))
            if prior is None:
                tops[pair] = top
                totals[pair] = jnp.zeros((2 * TOKENS, LANES), jnp.float32)
                sums[pair] = jnp.zeros((2 * TOKENS, LANES), jnp.float32)
            else:
                top = jnp.maximum(top, prior[pair])
                tops[pair] = top
                factor = jnp.exp(prior[pair] - top)
                totals[pair] = prior[PAIRS + pair] * factor
                sums[pair] = prior[2 * PAIRS + pair] * factor

        def mix(turn, carry):
            _, place = step_of(turn)
            start = pl.multiple_of(place * CHUNK, CHUNK)
            for pair in range(PAIRS):
                found = scores[turn, pair]
                left = jnp.exp(found[:, :LANES] - tops[pair])
                right = jnp.exp(found[:, LANES:] - tops[pair])
                totals[pair] = totals[pair] + (left + right)
                weights = jnp.concatenate([left, right], axis=1).astype(jnp.bfloat16)
                values = kv[
                    pl.ds(start, CHUNK), WIDTH + pair * LANES : WIDTH + (pair + 1) * LANES
                ]
                sums[pair] = sums[pair] + jnp.dot(
                    weights, values, preferred_element_type=jnp.float32
                )
            return carry

        lax.fori_loop(0, count, mix, 0)


def query_place(pair):
    return 3 * PAIRS + pair // 2, slice(pair % 2 * TOKENS, (pair % 2 + 1) * TOKENS)


def local_kernel(lengths_ref, place_ref, own, next_piece, far, last, *rest):
    out, (kv, queries, scores, states, sems) = rest[0], rest[1:]
    attention = Attention(lengths_ref, place_ref)
    pieces = (own, next_piece, far, last)
    asks, copies = [], []
    for turn in range(4):
        slot = lax.rem(attention.y + turn, 4)
        asks.append(
            pltpu.make_async_copy(
                pieces[turn].at[:, pl.ds(0, WIDTH)], queries.at[turn], sems.at[4 + turn]
            )
        )
        copies.append(
            pltpu.make_async_copy(
                pieces[turn].at[:, pl.ds(WIDTH, 2 * WIDTH)],
                kv.at[pl.ds(pl.multiple_of(slot * TOKENS, TOKENS), TOKENS)],
                sems.at[turn],
            )
        )
    for copy in asks + copies:
        copy.start()
    for copy in asks + copies:
        copy.wait()
    stores = []
    for i, offset in enumerate((2, 1, 3, 0)):
        if i >= 2:
            stores[i - 2].wait()
        which = lax.rem(attention.y + offset, 4)
        start, stop = attention.steps_of(which)
        start, stop = jnp.maximum(start, 2), jnp.minimum(stop, 4)
        state = states.at[i % 2]
        asked = [queries[offset, :, pair * LANES : (pair + 1) * LANES] for pair in range(PAIRS)]
        for pair in range(PAIRS):
            state[query_place(pair)] = asked[pair].astype(jnp.float32)
        attention.attend(
            which, asked, kv,
            lambda turn: (start + turn, start + turn - 2), stop - start,
            scores, state,
        )
        stores.append(pltpu.make_async_copy(state, out.at[offset], sems.at[8 + i]))
        stores[i].start()
    stores[2].wait()
    stores[3].wait()


def project(mixed, weights_ref, store):
    for tile in range(8):
        high, place = divmod(tile, 4)
        both = jnp.concatenate([weights_ref[0, place, high], weights_ref[1, place, high]], axis=1)
        store(tile * PAIR, jnp.dot(mixed, both, preferred_element_type=jnp.float32))


PAIR = 2 * LANES


def rows_kernel(
    offset, lengths_ref, place_ref, own_weights, other_weights,
    own_before, rest_before, own_after, rest_after, prior_hbm, out_ref,
    kv, prior, scores, state, weights, mixed, sems,
):
    core = place_ref[2]
    fetches = [
        pltpu.make_async_copy(own_weights, weights.at[core], sems.at[8]),
        pltpu.make_async_copy(other_weights, weights.at[1 - core], sems.at[9]),
    ]
    attention = Attention(lengths_ref, place_ref)
    which = lax.rem(attention.y + offset, 4)
    start, stop = attention.steps_of(which)
    ahead = jnp.maximum(2 - start, 0)
    behind = jnp.maximum(stop - 4, 0)
    copies = []
    for side, (first, others) in enumerate(((own_before, rest_before), (own_after, rest_after))):
        for turn in range(4):
            slot = lax.rem(attention.y + turn, 4)
            half = lax.div(slot, 2)
            copy = pltpu.make_async_copy(
                others.at[pl.ds((turn - 1) * TOKENS, TOKENS)] if turn else first,
                kv.at[pl.ds(pl.multiple_of((4 * side + slot) * TOKENS, TOKENS), TOKENS)],
                sems.at[4 * side + turn],
            )
            copies.append((half < behind if side else half >= 2 - ahead, copy))
    asked, rest = pl.ds(3 * PAIRS, 2), pl.ds(0, 3 * PAIRS)
    ask = pltpu.make_async_copy(prior_hbm.at[offset, asked], prior.at[asked], sems.at[10])
    recall = pltpu.make_async_copy(prior_hbm.at[offset, rest], prior.at[rest], sems.at[11])
    ask.start()
    for wanted, copy in copies:
        @pl.when(wanted)
        def _():
            copy.start()
    recall.start()
    for fetch in fetches:
        fetch.start()
    ask.wait()
    for wanted, copy in copies:
        @pl.when(wanted)
        def _():
            copy.wait()

    def step_of(turn):
        early = turn < ahead
        step = jnp.where(early, 2 - ahead + turn, 4 + turn - ahead)
        return step, jnp.where(early, step, step - 2)

    queries = [prior[query_place(pair)].astype(jnp.bfloat16) for pair in range(PAIRS)]
    attention.attend(
        which, queries, kv, step_of, ahead + behind, scores, state, prior, recall.wait
    )
    for pair in range(PAIRS):
        row_total = jnp.sum(state[PAIRS + pair], axis=1, keepdims=True)
        found = state[2 * PAIRS + pair] / row_total
        mixed[:, pair * LANES : (pair + 1) * LANES] = jnp.where(
            attention.low, found[:TOKENS], found[TOKENS:]
        ).astype(jnp.bfloat16)
    for fetch in fetches:
        fetch.wait()

    def store(start, value):
        out_ref[:, start : start + PAIR] = value.astype(out_ref.dtype)

    project(mixed[...], weights, store)


def finish_kernel(own_ref, one_ref, two_ref, three_ref, resid_ref, earlier_ref, out_ref):
    branch = own_ref[...] + one_ref[...].astype(jnp.float32)
    branch = branch + two_ref[...].astype(jnp.float32)
    branch = branch + three_ref[...].astype(jnp.float32)
    summed = resid_ref[...].astype(jnp.float32) + branch * (1.0 / math.sqrt(D))
    centered = summed - jnp.mean(summed, axis=1, keepdims=True)
    spread = jnp.mean(centered * centered, axis=1, keepdims=True)
    normed = centered * lax.rsqrt(spread + norm_epsilon)
    out_ref[...] = (earlier_ref[...] + normed) * (1.0 / TOP_K)


vmem = pl.BlockSpec(memory_space=pltpu.VMEM)
smem = pl.BlockSpec(memory_space=pltpu.SMEM)
anywhere = pl.BlockSpec(memory_space=pl.ANY)
running = (3 * PAIRS + 2, 2 * TOKENS, LANES)
local_scratch = [
    pltpu.VMEM((ROW, 2 * WIDTH), jnp.bfloat16),
    pltpu.VMEM((4, TOKENS, WIDTH), jnp.bfloat16),
    pltpu.VMEM((2, PAIRS, 2 * TOKENS, CHUNK), jnp.float32),
    pltpu.VMEM((2,) + running, jnp.float32),
    pltpu.SemaphoreType.DMA((12,)),
]
rows_scratch = [
    pltpu.VMEM((2 * ROW, 2 * WIDTH), jnp.bfloat16),
    pltpu.VMEM(running, jnp.float32),
    pltpu.VMEM((4, PAIRS, 2 * TOKENS, CHUNK), jnp.float32),
    pltpu.VMEM(running, jnp.float32),
    pltpu.VMEM((2, 4, 2, ROW, LANES), jnp.bfloat16),
    pltpu.VMEM((TOKENS, WIDTH), jnp.bfloat16),
    pltpu.SemaphoreType.DMA((12,)),
]


def cost(flops, moved, exps=0):
    return pl.CostEstimate(flops=flops, bytes_accessed=moved, transcendentals=exps)


def limit(mebibytes):
    return pltpu.CompilerParams(vmem_limit_bytes=mebibytes << 20)


def array(*shape, dtype=jnp.bfloat16):
    return jax.ShapeDtypeStruct(shape, dtype)


def shift(value, amount, axis="y", size=4):
    return lax.ppermute(value, axis, [(i, (i + amount) % size) for i in range(size)])


def block(qkv, resid, earlier, lengths, teacher_out, student_out):
    teacher_new = (
        ema_decay * teacher_out.astype(jnp.float32)
        + (1.0 - ema_decay) * student_out.astype(jnp.float32)
    ).astype(jnp.bfloat16)
    place = jnp.stack([lax.axis_index(name) for name in ("z", "y", "c")]).astype(jnp.int32)

    pack = pl.pallas_call(
        pack_kernel,
        grid=(TOKENS // PACKED,),
        out_shape=(array(TOKENS, 3 * WIDTH),) * 4,
        in_specs=[smem, pl.BlockSpec((PACKED, 3 * D), lambda i: (i, 0))],
        out_specs=(pl.BlockSpec((PACKED, 3 * WIDTH), lambda i: (i, 0)),) * 4,
        compiler_params=limit(12),
        cost_estimate=cost(0, 3 << 20),
        name="pack",
    )
    packed = pack(place, qkv[0])

    pieces = [packed[0]]
    for turn in (1, 2, 3):
        pieces.append(shift(packed[turn], -turn))
    ring = 2 * lax.axis_size("z")
    own_after = shift(packed[0][:, WIDTH:], -1, ("h", "z"), ring)
    own_before = shift(packed[0][:, WIDTH:], 1, ("h", "z"), ring)
    keys = jnp.concatenate([piece[:, WIDTH:] for piece in pieces[1:]], axis=0)
    rest_after = shift(keys, -1, ("h", "z"), ring)
    rest_before = shift(keys, 1, ("h", "z"), ring)

    ring_weights = lax.all_to_all(
        jnp.broadcast_to(teacher_new[None], (16,) + teacher_new.shape), ("h", "z"), 0, 0, tiled=True
    )
    ring_weights = ring_weights.reshape(2, ROW, LANES)
    own_weights = lax.all_to_all(
        jnp.broadcast_to(ring_weights[None], (4,) + ring_weights.shape), "x", 0, 0, tiled=True
    )
    other_weights = shift(own_weights, 1, "c", 2)

    local = pl.pallas_call(
        local_kernel,
        out_shape=array(4, *running, dtype=jnp.float32),
        in_specs=[smem, smem] + [anywhere] * 4,
        out_specs=anywhere,
        scratch_shapes=local_scratch,
        compiler_params=limit(16),
        cost_estimate=cost(1 << 30, 8 << 20, 2 << 20),
        name="local",
    )(lengths, place, *pieces)

    def rows_of(offset, dtype):
        return pl.pallas_call(
            functools.partial(rows_kernel, offset),
            out_shape=array(TOKENS, D, dtype=dtype),
            in_specs=[smem, smem] + [anywhere] * 7,
            out_specs=vmem,
            scratch_shapes=rows_scratch,
            compiler_params=limit(48),
            cost_estimate=cost(1 << 29, 4 << 20, 1 << 20),
            name="rows",
        )(
            lengths, place, own_weights, other_weights,
            own_before, rest_before, own_after, rest_after, local,
        )

    arrived = []
    for offset in (2, 1, 3):
        part = rows_of(offset, jnp.bfloat16)
        arrived.append(shift(part, offset))
    own = rows_of(0, jnp.float32)
    rows = pl.BlockSpec((32, D), lambda i: (i, 0))
    targets = pl.pallas_call(
        finish_kernel,
        grid=(4,),
        out_shape=array(TOKENS, D, dtype=jnp.float32),
        in_specs=[rows] * 6,
        out_specs=rows,
        compiler_params=limit(12),
        cost_estimate=cost(1 << 22, 5 << 20),
        name="finish",
    )(own, *arrived, resid[0], earlier[0])
    return (targets[None], teacher_new)


def solution(mesh):
    fine = Mesh(
        mesh.devices.reshape(2, 4, 2, 8, 4), ("h", "x", "c", "z", "y")
    )
    packs, frames = ("h", "x", "c"), ("z", "y")
    placed = (
        P(packs, frames, None),
        P(packs, frames, None),
        P(packs, frames, None),
        P(packs, None),
        P(frames, packs),
        P(frames, packs),
    )
    return jax.shard_map(
        block,
        mesh=fine,
        in_specs=placed,
        out_specs=(P(packs, frames, None), P(frames, packs)),
        check_vma=False,
    )
```

```python
import functools
import math

import jax
import jax.numpy as jnp
from jax import lax
from jax.experimental import pallas as pl
from jax.experimental.pallas import tpu as pltpu
from jax.sharding import Mesh, PartitionSpec as P

D = 2048
HEAD_DIM = 64
TOP_K = 8
UTTS = 12
LANES = 128
TOKENS = 128
ROW = 512
WIDTH = 512
CHUNK = 256
PAIRS = WIDTH // LANES
LOCAL_LIMIT = 58
ROWS_LIMIT = 48
PACKED = 32

ema_decay = 0.9
norm_epsilon = 1e-05
masked_score = -1e30


def pack_kernel(place_ref, qkv_ref, *outs):
    y = place_ref[1]
    low = lax.broadcasted_iota(jnp.int32, (PACKED, LANES), 1) < HEAD_DIM
    for turn in range(4):
        target = lax.rem(y + 4 - turn, 4)
        odd = lax.rem(target, 2) == 1
        half = lax.div(target, 2) * LANES
        for part in range(3):
            for pair in range(PAIRS):
                base = part * D + pair * 512
                first = qkv_ref[:, pl.ds(pl.multiple_of(base + half, LANES), LANES)].astype(jnp.float32)
                second = qkv_ref[:, pl.ds(pl.multiple_of(base + 256 + half, LANES), LANES)].astype(jnp.float32)
                left = jnp.where(odd, pltpu.roll(first, HEAD_DIM, 1), first)
                right = jnp.where(odd, second, pltpu.roll(second, HEAD_DIM, 1))
                both = jnp.where(low, left, right)
                if part == 0:
                    both = both * (1.0 / math.sqrt(HEAD_DIM))
                start = part * WIDTH + pair * LANES
                outs[turn][:, start : start + LANES] = both.astype(jnp.bfloat16)


class Attention:
    def __init__(self, lengths_ref, place_ref):
        self.row_start = place_ref[0] * ROW
        self.y = place_ref[1]
        self.base = self.row_start - ROW
        self.ends = []
        total = jnp.int32(0)
        for j in range(UTTS):
            total = total + lengths_ref[0, j]
            self.ends.append(total)
        self.low = lax.broadcasted_iota(jnp.int32, (TOKENS, LANES), 1) < HEAD_DIM
        self.middle = lax.broadcasted_iota(jnp.int32, (2 * TOKENS, LANES), 1) == HEAD_DIM

    def steps_of(self, which):
        first = self.row_start + which * TOKENS
        last = first + TOKENS - 1
        begin = jnp.int32(0)
        finish = jnp.int32(0)
        for end in reversed(self.ends):
            finish = jnp.where(end > last, end, finish)
        for end in self.ends:
            begin = jnp.where(end <= first, end, begin)
        return lax.div(begin - self.base, CHUNK), lax.div(finish - self.base + CHUNK - 1, CHUNK)

    def segments(self, frames):
        found = jnp.zeros(frames.shape, jnp.int32)
        for end in self.ends:
            found = found + (frames >= end).astype(jnp.int32)
        return jnp.where(frames < 0, -1, found)

    def attend(self, which, queries, kv, step_of, count, scores, state, prior=None):
        low = self.low
        tops, totals, sums = (state.at[pl.ds(PAIRS * i, PAIRS)] for i in range(3))
        row_segment = self.segments(
            self.row_start + which * TOKENS + lax.broadcasted_iota(jnp.int32, (TOKENS, LANES), 0)
        )
        row_segment = jnp.concatenate([row_segment, row_segment], axis=1)
        stacked = []
        for pair in range(PAIRS):
            one = queries[pair]
            zero = jnp.zeros_like(one)
            stacked.append(
                jnp.concatenate([jnp.where(low, one, zero), jnp.where(low, zero, one)], axis=0)
            )
        tops[...] = jnp.full(tops.shape, masked_score, jnp.float32)

        def score(turn, carry):
            step, place = step_of(turn)
            start = pl.multiple_of(place * CHUNK, CHUNK)
            key_segment = self.segments(
                self.base + step * CHUNK + lax.broadcasted_iota(jnp.int32, (8, CHUNK), 1)
            )[:1]
            allowed = row_segment == key_segment
            allowed = jnp.concatenate([allowed, allowed], axis=0)
            for pair in range(PAIRS):
                keys = kv[pl.ds(start, CHUNK), pair * LANES : (pair + 1) * LANES]
                found = lax.dot_general(
                    stacked[pair], keys, (((1,), (1,)), ((), ())),
                    preferred_element_type=jnp.float32,
                )
                found = jnp.where(allowed, found, masked_score)
                scores[turn, pair] = found
                tops[pair] = jnp.maximum(
                    tops[pair], jnp.maximum(found[:, :LANES], found[:, LANES:])
                )
            return carry

        lax.fori_loop(0, count, score, 0)
        for pair in range(PAIRS):
            top = jnp.max(tops[pair], axis=1, keepdims=True)
            top = jnp.broadcast_to(top, (2 * TOKENS, LANES))
            if prior is None:
                tops[pair] = top
                totals[pair] = jnp.zeros((2 * TOKENS, LANES), jnp.float32)
                sums[pair] = jnp.zeros((2 * TOKENS, LANES), jnp.float32)
            else:
                stats = jnp.concatenate([prior[2 * pair], prior[2 * pair + 1]], axis=0)
                old = jnp.broadcast_to(stats[:, :1], (2 * TOKENS, LANES))
                top = jnp.maximum(top, old)
                tops[pair] = top
                factor = jnp.exp(old - top)
                totals[pair] = jnp.where(self.middle, stats * factor, 0.0)
                known = prior[2 * PAIRS + pair]
                sums[pair] = jnp.concatenate([known, known], axis=0) * factor

        def mix(turn, carry):
            _, place = step_of(turn)
            start = pl.multiple_of(place * CHUNK, CHUNK)
            for pair in range(PAIRS):
                found = scores[turn, pair]
                left = jnp.exp(found[:, :LANES] - tops[pair])
                right = jnp.exp(found[:, LANES:] - tops[pair])
                totals[pair] = totals[pair] + (left + right)
                weights = jnp.concatenate([left, right], axis=1).astype(jnp.bfloat16)
                values = kv[
                    pl.ds(start, CHUNK), WIDTH + pair * LANES : WIDTH + (pair + 1) * LANES
                ]
                sums[pair] = sums[pair] + jnp.dot(
                    weights, values, preferred_element_type=jnp.float32
                )
            return carry

        lax.fori_loop(0, count, mix, 0)


def local_kernel(lengths_ref, place_ref, own, next_piece, far, last, out, *rest):
    kv, queries, scores, state, packed, sems = rest
    attention = Attention(lengths_ref, place_ref)
    pieces = (own, next_piece, far, last)
    asks, copies = [], []
    for turn in range(4):
        slot = lax.rem(attention.y + turn, 4)
        asks.append(
            pltpu.make_async_copy(
                pieces[turn].at[:, pl.ds(0, WIDTH)], queries.at[turn], sems.at[4 + turn]
            )
        )
        copies.append(
            pltpu.make_async_copy(
                pieces[turn].at[:, pl.ds(WIDTH, 2 * WIDTH)],
                kv.at[pl.ds(pl.multiple_of(slot * TOKENS, TOKENS), TOKENS)],
                sems.at[turn],
            )
        )
    for copy in asks + copies:
        copy.start()
    for copy in asks + copies:
        copy.wait()
    stores = []
    for i, offset in enumerate((2, 1, 3, 0)):
        which = lax.rem(attention.y + offset, 4)
        start, stop = attention.steps_of(which)
        start, stop = jnp.maximum(start, 2), jnp.minimum(stop, 4)
        asked = [queries[offset, :, pair * LANES : (pair + 1) * LANES] for pair in range(PAIRS)]
        attention.attend(
            which, asked, kv,
            lambda turn: (start + turn, start + turn - 2), stop - start,
            scores, state,
        )
        if i >= 2:
            stores[i - 2].wait()
        tiles = packed.at[i % 2]
        for pair in range(PAIRS):
            total = jnp.sum(state[PAIRS + pair], axis=1, keepdims=True)
            total = jnp.broadcast_to(total, (2 * TOKENS, LANES))
            top, found = state[pair], state[2 * PAIRS + pair]
            tiles[2 * pair] = jnp.where(attention.low, top[:TOKENS], total[:TOKENS])
            tiles[2 * pair + 1] = jnp.where(attention.low, top[TOKENS:], total[TOKENS:])
            tiles[2 * PAIRS + pair] = jnp.where(attention.low, found[:TOKENS], found[TOKENS:])
            tiles[3 * PAIRS + pair] = asked[pair].astype(jnp.float32)
        stores.append(pltpu.make_async_copy(tiles, out.at[offset], sems.at[8 + i]))
        stores[i].start()
    stores[2].wait()
    stores[3].wait()


def project(mixed, core, own_weights, other_weights, store):
    for tile in range(8):
        high, place = divmod(tile, 4)
        both = jnp.concatenate([own_weights[place, high], other_weights[place, high]], axis=1)
        found = jnp.dot(mixed, both, preferred_element_type=jnp.float32)
        start = tile * 2 * LANES
        store(pl.multiple_of(start + core * LANES, LANES), found[:, :LANES])
        store(pl.multiple_of(start + (1 - core) * LANES, LANES), found[:, LANES:])


def rows_kernel(
    offsets, lengths_ref, place_ref, own_weights, other_weights, before, after, prior_hbm, *rest
):
    outs, (kv, priors, scores, state, mixed, sems) = rest[: len(offsets)], rest[len(offsets) :]
    attention = Attention(lengths_ref, place_ref)
    whiches, aheads, behinds, recalls = [], [], [], []
    for i, offset in enumerate(offsets):
        which = lax.rem(attention.y + offset, 4)
        start, stop = attention.steps_of(which)
        whiches.append(which)
        aheads.append(jnp.maximum(2 - start, 0))
        behinds.append(jnp.maximum(stop - 4, 0))
        recalls.append(pltpu.make_async_copy(prior_hbm.at[offset], priors.at[i], sems.at[8 + i]))
    recalls[0].start()
    most_ahead = functools.reduce(jnp.maximum, aheads)
    most_behind = functools.reduce(jnp.maximum, behinds)
    copies = []
    for side, source in enumerate((before, after)):
        for turn in range(4):
            slot = lax.rem(attention.y + turn, 4)
            half = lax.div(slot, 2)
            copy = pltpu.make_async_copy(
                source.at[pl.ds(turn * TOKENS, TOKENS)],
                kv.at[pl.ds(pl.multiple_of((4 * side + slot) * TOKENS, TOKENS), TOKENS)],
                sems.at[4 * side + turn],
            )
            copies.append((half < most_behind if side else half >= 2 - most_ahead, copy))
    for wanted, copy in copies:
        @pl.when(wanted)
        def _():
            copy.start()
    for recall in recalls[1:]:
        recall.start()
    for wanted, copy in copies:
        @pl.when(wanted)
        def _():
            copy.wait()
    for i, which in enumerate(whiches):
        ahead, behind, prior = aheads[i], behinds[i], priors.at[i]
        recalls[i].wait()

        def step_of(turn):
            early = turn < ahead
            step = jnp.where(early, 2 - ahead + turn, 4 + turn - ahead)
            return step, jnp.where(early, step, step - 2)

        queries = [prior[3 * PAIRS + pair].astype(jnp.bfloat16) for pair in range(PAIRS)]
        attention.attend(which, queries, kv, step_of, ahead + behind, scores, state, prior)
        for pair in range(PAIRS):
            row_total = jnp.sum(state[PAIRS + pair], axis=1, keepdims=True)
            found = state[2 * PAIRS + pair] / row_total
            mixed[i * TOKENS : (i + 1) * TOKENS, pair * LANES : (pair + 1) * LANES] = jnp.where(
                attention.low, found[:TOKENS], found[TOKENS:]
            ).astype(jnp.bfloat16)

    def store(start, value):
        for i, out_ref in enumerate(outs):
            part = value[i * TOKENS : (i + 1) * TOKENS]
            out_ref[:, pl.ds(start, LANES)] = part.astype(out_ref.dtype)

    project(mixed[...], place_ref[2], own_weights, other_weights, store)


def finish_kernel(own_ref, one_ref, two_ref, three_ref, resid_ref, earlier_ref, out_ref):
    branch = own_ref[...] + one_ref[...].astype(jnp.float32)
    branch = branch + two_ref[...].astype(jnp.float32)
    branch = branch + three_ref[...].astype(jnp.float32)
    summed = resid_ref[...].astype(jnp.float32) + branch * (1.0 / math.sqrt(D))
    centered = summed - jnp.mean(summed, axis=1, keepdims=True)
    spread = jnp.mean(centered * centered, axis=1, keepdims=True)
    normed = centered * lax.rsqrt(spread + norm_epsilon)
    out_ref[...] = (earlier_ref[...] + normed) * (1.0 / TOP_K)


vmem = pl.BlockSpec(memory_space=pltpu.VMEM)
smem = pl.BlockSpec(memory_space=pltpu.SMEM)
anywhere = pl.BlockSpec(memory_space=pl.ANY)
running = (3 * PAIRS, 2 * TOKENS, LANES)
handed = (4 * PAIRS, TOKENS, LANES)
local_scratch = [
    pltpu.VMEM((ROW, 2 * WIDTH), jnp.bfloat16),
    pltpu.VMEM((4, TOKENS, WIDTH), jnp.bfloat16),
    pltpu.VMEM((2, PAIRS, 2 * TOKENS, CHUNK), jnp.float32),
    pltpu.VMEM(running, jnp.float32),
    pltpu.VMEM((2,) + handed, jnp.float32),
    pltpu.SemaphoreType.DMA((12,)),
]


def cost(flops, moved, exps=0):
    return pl.CostEstimate(flops=flops, bytes_accessed=moved, transcendentals=exps)


def limit(mebibytes):
    return pltpu.CompilerParams(vmem_limit_bytes=mebibytes << 20)


def array(*shape, dtype=jnp.bfloat16):
    return jax.ShapeDtypeStruct(shape, dtype)


def shift(value, amount, axis="y", size=4):
    return lax.ppermute(value, axis, [(i, (i + amount) % size) for i in range(size)])


def block(qkv, resid, earlier, lengths, teacher_out, student_out):
    teacher_new = (
        ema_decay * teacher_out.astype(jnp.float32)
        + (1.0 - ema_decay) * student_out.astype(jnp.float32)
    ).astype(jnp.bfloat16)
    place = jnp.stack([lax.axis_index(name) for name in ("z", "y", "c")]).astype(jnp.int32)

    pack = pl.pallas_call(
        pack_kernel,
        grid=(TOKENS // PACKED,),
        out_shape=(array(TOKENS, 3 * WIDTH),) * 4,
        in_specs=[smem, pl.BlockSpec((PACKED, 3 * D), lambda i: (i, 0))],
        out_specs=(pl.BlockSpec((PACKED, 3 * WIDTH), lambda i: (i, 0)),) * 4,
        compiler_params=limit(12),
        cost_estimate=cost(0, 3 << 20),
        name="pack",
    )
    packed = pack(place, qkv[0])

    pieces = [packed[0]]
    for turn in (1, 2, 3):
        pieces.append(shift(packed[turn], -turn))
    ring = 2 * lax.axis_size("z")
    keys = jnp.concatenate([piece[:, WIDTH:] for piece in pieces], axis=0)
    after = shift(keys, -1, ("h", "z"), ring)
    before = shift(keys, 1, ("h", "z"), ring)

    ring_weights = lax.all_to_all(
        jnp.broadcast_to(teacher_new[None], (16,) + teacher_new.shape), ("h", "z"), 0, 0, tiled=True
    )
    ring_weights = ring_weights.reshape(2, ROW, LANES)
    own_weights = lax.all_to_all(
        jnp.broadcast_to(ring_weights[None], (4,) + ring_weights.shape), "x", 0, 0, tiled=True
    )
    other_weights = shift(own_weights, 1, "c", 2)

    local = pl.pallas_call(
        local_kernel,
        out_shape=array(4, *handed, dtype=jnp.float32),
        in_specs=[smem, smem] + [anywhere] * 4,
        out_specs=anywhere,
        scratch_shapes=local_scratch,
        compiler_params=limit(LOCAL_LIMIT),
        cost_estimate=cost(1 << 30, 8 << 20, 2 << 20),
        name="local",
    )(lengths, place, *pieces)

    def rows_of(offsets, dtype):
        count = len(offsets)
        return pl.pallas_call(
            functools.partial(rows_kernel, offsets),
            out_shape=(array(TOKENS, D, dtype=dtype),) * count,
            in_specs=[smem, smem, vmem, vmem] + [anywhere] * 3,
            out_specs=(vmem,) * count,
            scratch_shapes=[
                pltpu.VMEM((2 * ROW, 2 * WIDTH), jnp.bfloat16),
                pltpu.VMEM((count,) + handed, jnp.float32),
                pltpu.VMEM((4, PAIRS, 2 * TOKENS, CHUNK), jnp.float32),
                pltpu.VMEM(running, jnp.float32),
                pltpu.VMEM((count * TOKENS, WIDTH), jnp.bfloat16),
                pltpu.SemaphoreType.DMA((10,)),
            ],
            compiler_params=limit(ROWS_LIMIT),
            cost_estimate=cost(count << 29, 4 << 20, count << 20),
            name="rows",
        )(lengths, place, own_weights, other_weights, before, after, local)

    (far,) = rows_of((2,), jnp.bfloat16)
    far = shift(far, 2)
    up, down = rows_of((1, 3), jnp.bfloat16)
    up = shift(up, 1)
    down = shift(down, 3)
    (own,) = rows_of((0,), jnp.float32)
    rows = pl.BlockSpec((32, D), lambda i: (i, 0))
    targets = pl.pallas_call(
        finish_kernel,
        grid=(4,),
        out_shape=array(TOKENS, D, dtype=jnp.float32),
        in_specs=[rows] * 6,
        out_specs=rows,
        compiler_params=limit(12),
        cost_estimate=cost(1 << 22, 5 << 20),
        name="finish",
    )(own, far, up, down, resid[0], earlier[0])
    return (targets[None], teacher_new)


def solution(mesh):
    fine = Mesh(
        mesh.devices.reshape(2, 4, 2, 8, 4), ("h", "x", "c", "z", "y")
    )
    packs, frames = ("h", "x", "c"), ("z", "y")
    placed = (
        P(packs, frames, None),
        P(packs, frames, None),
        P(packs, frames, None),
        P(packs, None),
        P(frames, packs),
        P(frames, packs),
    )
    return jax.shard_map(
        block,
        mesh=fine,
        in_specs=placed,
        out_specs=(P(packs, frames, None), P(frames, packs)),
        check_vma=False,
    )
```

```python
import functools
import math

import jax
import jax.numpy as jnp
from jax import lax
from jax.experimental import pallas as pl
from jax.experimental.pallas import tpu as pltpu
from jax.sharding import Mesh, PartitionSpec as P

D = 2048
HEAD_DIM = 64
TOP_K = 8
UTTS = 12
LANES = 128
TOKENS = 128
ROW = 512
WIDTH = 512
CHUNK = 256
PAIRS = WIDTH // LANES
LOCAL_LIMIT = 58
ROWS_LIMIT = 24
PACKED = 32

ema_decay = 0.9
norm_epsilon = 1e-05
masked_score = -1e30


def pack_kernel(place_ref, qkv_ref, *outs):
    y = place_ref[1]
    low = lax.broadcasted_iota(jnp.int32, (PACKED, LANES), 1) < HEAD_DIM
    for turn in range(4):
        target = lax.rem(y + 4 - turn, 4)
        odd = lax.rem(target, 2) == 1
        half = lax.div(target, 2) * LANES
        for part in range(3):
            for pair in range(PAIRS):
                base = part * D + pair * 512
                first = qkv_ref[:, pl.ds(pl.multiple_of(base + half, LANES), LANES)].astype(jnp.float32)
                second = qkv_ref[:, pl.ds(pl.multiple_of(base + 256 + half, LANES), LANES)].astype(jnp.float32)
                left = jnp.where(odd, pltpu.roll(first, HEAD_DIM, 1), first)
                right = jnp.where(odd, second, pltpu.roll(second, HEAD_DIM, 1))
                both = jnp.where(low, left, right)
                if part == 0:
                    both = both * (1.0 / math.sqrt(HEAD_DIM))
                start = part * WIDTH + pair * LANES
                outs[turn][:, start : start + LANES] = both.astype(jnp.bfloat16)


class Attention:
    def __init__(self, lengths_ref, place_ref):
        self.row_start = place_ref[0] * ROW
        self.y = place_ref[1]
        self.base = self.row_start - ROW
        self.ends = []
        total = jnp.int32(0)
        for j in range(UTTS):
            total = total + lengths_ref[0, j]
            self.ends.append(total)
        self.low = lax.broadcasted_iota(jnp.int32, (TOKENS, LANES), 1) < HEAD_DIM
        self.middle = lax.broadcasted_iota(jnp.int32, (2 * TOKENS, LANES), 1) == HEAD_DIM

    def steps_of(self, which):
        first = self.row_start + which * TOKENS
        last = first + TOKENS - 1
        begin = jnp.int32(0)
        finish = jnp.int32(0)
        for end in reversed(self.ends):
            finish = jnp.where(end > last, end, finish)
        for end in self.ends:
            begin = jnp.where(end <= first, end, begin)
        return lax.div(begin - self.base, CHUNK), lax.div(finish - self.base + CHUNK - 1, CHUNK)

    def segments(self, frames):
        found = jnp.zeros(frames.shape, jnp.int32)
        for end in self.ends:
            found = found + (frames >= end).astype(jnp.int32)
        return jnp.where(frames < 0, -1, found)

    def attend(self, which, queries, kv, step_of, count, scores, state, prior=None):
        low = self.low
        tops, totals, sums = (state.at[pl.ds(PAIRS * i, PAIRS)] for i in range(3))
        row_segment = self.segments(
            self.row_start + which * TOKENS + lax.broadcasted_iota(jnp.int32, (TOKENS, LANES), 0)
        )
        row_segment = jnp.concatenate([row_segment, row_segment], axis=1)
        stacked = []
        for pair in range(PAIRS):
            one = queries[pair]
            zero = jnp.zeros_like(one)
            stacked.append(
                jnp.concatenate([jnp.where(low, one, zero), jnp.where(low, zero, one)], axis=0)
            )
        tops[...] = jnp.full(tops.shape, masked_score, jnp.float32)

        def score(turn, carry):
            step, place = step_of(turn)
            start = pl.multiple_of(place * CHUNK, CHUNK)
            key_segment = self.segments(
                self.base + step * CHUNK + lax.broadcasted_iota(jnp.int32, (8, CHUNK), 1)
            )[:1]
            allowed = row_segment == key_segment
            allowed = jnp.concatenate([allowed, allowed], axis=0)
            for pair in range(PAIRS):
                keys = kv[pl.ds(start, CHUNK), pair * LANES : (pair + 1) * LANES]
                found = lax.dot_general(
                    stacked[pair], keys, (((1,), (1,)), ((), ())),
                    preferred_element_type=jnp.float32,
                )
                found = jnp.where(allowed, found, masked_score)
                scores[turn, pair] = found
                tops[pair] = jnp.maximum(
                    tops[pair], jnp.maximum(found[:, :LANES], found[:, LANES:])
                )
            return carry

        lax.fori_loop(0, count, score, 0)
        for pair in range(PAIRS):
            top = jnp.max(tops[pair], axis=1, keepdims=True)
            top = jnp.broadcast_to(top, (2 * TOKENS, LANES))
            if prior is None:
                tops[pair] = top
                totals[pair] = jnp.zeros((2 * TOKENS, LANES), jnp.float32)
                sums[pair] = jnp.zeros((2 * TOKENS, LANES), jnp.float32)
            else:
                stats = jnp.concatenate([prior[2 * pair], prior[2 * pair + 1]], axis=0)
                old = jnp.broadcast_to(stats[:, :1], (2 * TOKENS, LANES))
                top = jnp.maximum(top, old)
                tops[pair] = top
                factor = jnp.exp(old - top)
                totals[pair] = jnp.where(self.middle, stats * factor, 0.0)
                known = prior[2 * PAIRS + pair]
                sums[pair] = jnp.concatenate([known, known], axis=0) * factor

        def mix(turn, carry):
            _, place = step_of(turn)
            start = pl.multiple_of(place * CHUNK, CHUNK)
            for pair in range(PAIRS):
                found = scores[turn, pair]
                left = jnp.exp(found[:, :LANES] - tops[pair])
                right = jnp.exp(found[:, LANES:] - tops[pair])
                totals[pair] = totals[pair] + (left + right)
                weights = jnp.concatenate([left, right], axis=1).astype(jnp.bfloat16)
                values = kv[
                    pl.ds(start, CHUNK), WIDTH + pair * LANES : WIDTH + (pair + 1) * LANES
                ]
                sums[pair] = sums[pair] + jnp.dot(
                    weights, values, preferred_element_type=jnp.float32
                )
            return carry

        lax.fori_loop(0, count, mix, 0)


def local_kernel(lengths_ref, place_ref, own, next_piece, far, last, *rest):
    outs, (kv, queries, scores, state, packed, sems) = rest[:4], rest[4:]
    attention = Attention(lengths_ref, place_ref)
    pieces = (own, next_piece, far, last)
    asks, copies = [], []
    for turn in range(4):
        slot = lax.rem(attention.y + turn, 4)
        asks.append(
            pltpu.make_async_copy(
                pieces[turn].at[:, pl.ds(0, WIDTH)], queries.at[turn], sems.at[4 + turn]
            )
        )
        copies.append(
            pltpu.make_async_copy(
                pieces[turn].at[:, pl.ds(WIDTH, 2 * WIDTH)],
                kv.at[pl.ds(pl.multiple_of(slot * TOKENS, TOKENS), TOKENS)],
                sems.at[turn],
            )
        )
    for copy in asks + copies:
        copy.start()
    for copy in asks + copies:
        copy.wait()
    stores = []
    for i, offset in enumerate((2, 1, 3, 0)):
        which = lax.rem(attention.y + offset, 4)
        start, stop = attention.steps_of(which)
        start, stop = jnp.maximum(start, 2), jnp.minimum(stop, 4)
        asked = [queries[offset, :, pair * LANES : (pair + 1) * LANES] for pair in range(PAIRS)]
        attention.attend(
            which, asked, kv,
            lambda turn: (start + turn, start + turn - 2), stop - start,
            scores, state,
        )
        if i >= 2:
            stores[i - 2].wait()
        tiles = packed.at[i % 2]
        for pair in range(PAIRS):
            total = jnp.sum(state[PAIRS + pair], axis=1, keepdims=True)
            total = jnp.broadcast_to(total, (2 * TOKENS, LANES))
            top, found = state[pair], state[2 * PAIRS + pair]
            tiles[2 * pair] = jnp.where(attention.low, top[:TOKENS], total[:TOKENS])
            tiles[2 * pair + 1] = jnp.where(attention.low, top[TOKENS:], total[TOKENS:])
            tiles[2 * PAIRS + pair] = jnp.where(attention.low, found[:TOKENS], found[TOKENS:])
            tiles[3 * PAIRS + pair] = asked[pair].astype(jnp.float32)
        stores.append(pltpu.make_async_copy(tiles, outs[offset], sems.at[8 + i]))
        stores[i].start()
    stores[2].wait()
    stores[3].wait()


def project(mixed, core, own_weights, other_weights, store):
    for tile in range(8):
        high, place = divmod(tile, 4)
        both = jnp.concatenate([own_weights[place, high], other_weights[place, high]], axis=1)
        found = jnp.dot(mixed, both, preferred_element_type=jnp.float32)
        start = tile * 2 * LANES
        store(pl.multiple_of(start + core * LANES, LANES), found[:, :LANES])
        store(pl.multiple_of(start + (1 - core) * LANES, LANES), found[:, LANES:])


def attend_rows(offsets, lengths_ref, place_ref, before, after, priors, kv, scores, state, mixed, sems):
    attention = Attention(lengths_ref, place_ref)
    whiches, aheads, behinds = [], [], []
    for offset in offsets:
        which = lax.rem(attention.y + offset, 4)
        start, stop = attention.steps_of(which)
        whiches.append(which)
        aheads.append(jnp.maximum(2 - start, 0))
        behinds.append(jnp.maximum(stop - 4, 0))
    most_ahead = functools.reduce(jnp.maximum, aheads)
    most_behind = functools.reduce(jnp.maximum, behinds)
    copies = []
    for side, source in enumerate((before, after)):
        for turn in range(4):
            slot = lax.rem(attention.y + turn, 4)
            half = lax.div(slot, 2)
            copy = pltpu.make_async_copy(
                source.at[pl.ds(turn * TOKENS, TOKENS)],
                kv.at[pl.ds(pl.multiple_of((4 * side + slot) * TOKENS, TOKENS), TOKENS)],
                sems.at[4 * side + turn],
            )
            copies.append((half < most_behind if side else half >= 2 - most_ahead, copy))
    for wanted, copy in copies:
        @pl.when(wanted)
        def _():
            copy.start()
    for wanted, copy in copies:
        @pl.when(wanted)
        def _():
            copy.wait()
    for i, which in enumerate(whiches):
        ahead, behind, prior = aheads[i], behinds[i], priors[i]

        def step_of(turn):
            early = turn < ahead
            step = jnp.where(early, 2 - ahead + turn, 4 + turn - ahead)
            return step, jnp.where(early, step, step - 2)

        queries = [prior[3 * PAIRS + pair].astype(jnp.bfloat16) for pair in range(PAIRS)]
        attention.attend(which, queries, kv, step_of, ahead + behind, scores, state, prior)
        for pair in range(PAIRS):
            row_total = jnp.sum(state[PAIRS + pair], axis=1, keepdims=True)
            found = state[2 * PAIRS + pair] / row_total
            mixed[i * TOKENS : (i + 1) * TOKENS, pair * LANES : (pair + 1) * LANES] = jnp.where(
                attention.low, found[:TOKENS], found[TOKENS:]
            ).astype(jnp.bfloat16)


def attend_kernel(offsets, lengths_ref, place_ref, before, after, *rest):
    count = len(offsets)
    priors, (mixed, *scratch) = rest[:count], rest[count:]
    kv, scores, state, sems = scratch
    attend_rows(
        offsets, lengths_ref, place_ref, before, after, priors, kv, scores, state, mixed, sems
    )


def project_kernel(place_ref, own_weights, other_weights, mixed, out_ref):
    def store(start, value):
        out_ref[:, pl.ds(start, LANES)] = value.astype(out_ref.dtype)

    project(mixed[...], place_ref[2], own_weights, other_weights, store)


def rows_kernel(
    offsets, lengths_ref, place_ref, own_weights, other_weights, before, after, *rest
):
    count = len(offsets)
    priors, outs, scratch = rest[:count], rest[count : 2 * count], rest[2 * count :]
    kv, scores, state, sems, mixed = scratch
    attend_rows(
        offsets, lengths_ref, place_ref, before, after, priors, kv, scores, state, mixed, sems
    )

    def store(start, value):
        for i, out_ref in enumerate(outs):
            part = value[i * TOKENS : (i + 1) * TOKENS]
            out_ref[:, pl.ds(start, LANES)] = part.astype(out_ref.dtype)

    project(mixed[...], place_ref[2], own_weights, other_weights, store)


def finish_kernel(own_ref, one_ref, two_ref, three_ref, resid_ref, earlier_ref, out_ref):
    branch = own_ref[...] + one_ref[...].astype(jnp.float32)
    branch = branch + two_ref[...].astype(jnp.float32)
    branch = branch + three_ref[...].astype(jnp.float32)
    summed = resid_ref[...].astype(jnp.float32) + branch * (1.0 / math.sqrt(D))
    centered = summed - jnp.mean(summed, axis=1, keepdims=True)
    spread = jnp.mean(centered * centered, axis=1, keepdims=True)
    normed = centered * lax.rsqrt(spread + norm_epsilon)
    out_ref[...] = (earlier_ref[...] + normed) * (1.0 / TOP_K)


vmem = pl.BlockSpec(memory_space=pltpu.VMEM)
smem = pl.BlockSpec(memory_space=pltpu.SMEM)
anywhere = pl.BlockSpec(memory_space=pl.ANY)
running = (3 * PAIRS, 2 * TOKENS, LANES)
handed = (4 * PAIRS, TOKENS, LANES)
local_scratch = [
    pltpu.VMEM((ROW, 2 * WIDTH), jnp.bfloat16),
    pltpu.VMEM((4, TOKENS, WIDTH), jnp.bfloat16),
    pltpu.VMEM((2, PAIRS, 2 * TOKENS, CHUNK), jnp.float32),
    pltpu.VMEM(running, jnp.float32),
    pltpu.VMEM((2,) + handed, jnp.float32),
    pltpu.SemaphoreType.DMA((12,)),
]
rows_scratch = [
    pltpu.VMEM((2 * ROW, 2 * WIDTH), jnp.bfloat16),
    pltpu.VMEM((4, PAIRS, 2 * TOKENS, CHUNK), jnp.float32),
    pltpu.VMEM(running, jnp.float32),
    pltpu.SemaphoreType.DMA((8,)),
]


def cost(flops, moved, exps=0):
    return pl.CostEstimate(flops=flops, bytes_accessed=moved, transcendentals=exps)


def limit(mebibytes):
    return pltpu.CompilerParams(vmem_limit_bytes=mebibytes << 20)


def array(*shape, dtype=jnp.bfloat16):
    return jax.ShapeDtypeStruct(shape, dtype)


def shift(value, amount, axis="y", size=4):
    return lax.ppermute(value, axis, [(i, (i + amount) % size) for i in range(size)])


def block(qkv, resid, earlier, lengths, teacher_out, student_out):
    teacher_new = (
        ema_decay * teacher_out.astype(jnp.float32)
        + (1.0 - ema_decay) * student_out.astype(jnp.float32)
    ).astype(jnp.bfloat16)
    place = jnp.stack([lax.axis_index(name) for name in ("z", "y", "c")]).astype(jnp.int32)

    pack = pl.pallas_call(
        pack_kernel,
        grid=(TOKENS // PACKED,),
        out_shape=(array(TOKENS, 3 * WIDTH),) * 4,
        in_specs=[smem, pl.BlockSpec((PACKED, 3 * D), lambda i: (i, 0))],
        out_specs=(pl.BlockSpec((PACKED, 3 * WIDTH), lambda i: (i, 0)),) * 4,
        compiler_params=limit(12),
        cost_estimate=cost(0, 3 << 20),
        name="pack",
    )
    packed = pack(place, qkv[0])

    pieces = [packed[0]]
    for turn in (1, 2, 3):
        pieces.append(shift(packed[turn], -turn))
    ring = 2 * lax.axis_size("z")
    keys = jnp.concatenate([piece[:, WIDTH:] for piece in pieces], axis=0)
    after = shift(keys, -1, ("h", "z"), ring)
    before = shift(keys, 1, ("h", "z"), ring)

    ring_weights = lax.all_to_all(
        jnp.broadcast_to(teacher_new[None], (16,) + teacher_new.shape), ("h", "z"), 0, 0, tiled=True
    )
    ring_weights = ring_weights.reshape(2, ROW, LANES)
    own_weights = lax.all_to_all(
        jnp.broadcast_to(ring_weights[None], (4,) + ring_weights.shape), "x", 0, 0, tiled=True
    )
    other_weights = shift(own_weights, 1, "c", 2)

    local = pl.pallas_call(
        local_kernel,
        out_shape=(array(*handed, dtype=jnp.float32),) * 4,
        in_specs=[smem, smem] + [anywhere] * 4,
        out_specs=(anywhere,) * 4,
        scratch_shapes=local_scratch,
        compiler_params=limit(LOCAL_LIMIT),
        cost_estimate=cost(1 << 30, 8 << 20, 2 << 20),
        name="local",
    )(lengths, place, *pieces)

    def rows_of(offsets, dtype):
        count = len(offsets)
        return pl.pallas_call(
            functools.partial(rows_kernel, offsets),
            out_shape=(array(TOKENS, D, dtype=dtype),) * count,
            in_specs=[smem, smem, vmem, vmem, anywhere, anywhere] + [vmem] * count,
            out_specs=(vmem,) * count,
            scratch_shapes=rows_scratch + [pltpu.VMEM((count * TOKENS, WIDTH), jnp.bfloat16)],
            compiler_params=limit(ROWS_LIMIT),
            cost_estimate=cost(count << 29, 4 << 20, count << 20),
            name="rows",
        )(
            lengths, place, own_weights, other_weights, before, after,
            *[local[offset] for offset in offsets],
        )

    mixed = pl.pallas_call(
        functools.partial(attend_kernel, (2,)),
        out_shape=array(TOKENS, WIDTH),
        in_specs=[smem, smem, anywhere, anywhere, vmem],
        out_specs=vmem,
        scratch_shapes=rows_scratch,
        compiler_params=limit(ROWS_LIMIT),
        cost_estimate=cost(1 << 28, 3 << 20, 1 << 20),
        name="attend",
    )(lengths, place, before, after, local[2])
    far = pl.pallas_call(
        project_kernel,
        out_shape=array(TOKENS, D),
        in_specs=[smem, vmem, vmem, vmem],
        out_specs=vmem,
        compiler_params=limit(8),
        cost_estimate=cost(2 * TOKENS * WIDTH * D, 3 << 20),
        name="project",
    )(place, own_weights, other_weights, mixed)
    far = shift(far, 2)
    up, down = rows_of((1, 3), jnp.bfloat16)
    up = shift(up, 1)
    down = shift(down, 3)
    (own,) = rows_of((0,), jnp.float32)
    rows = pl.BlockSpec((32, D), lambda i: (i, 0))
    targets = pl.pallas_call(
        finish_kernel,
        grid=(4,),
        out_shape=array(TOKENS, D, dtype=jnp.float32),
        in_specs=[rows] * 6,
        out_specs=rows,
        compiler_params=limit(12),
        cost_estimate=cost(1 << 22, 5 << 20),
        name="finish",
    )(own, far, up, down, resid[0], earlier[0])
    return (targets[None], teacher_new)


def solution(mesh):
    fine = Mesh(
        mesh.devices.reshape(2, 4, 2, 8, 4), ("h", "x", "c", "z", "y")
    )
    packs, frames = ("h", "x", "c"), ("z", "y")
    placed = (
        P(packs, frames, None),
        P(packs, frames, None),
        P(packs, frames, None),
        P(packs, None),
        P(frames, packs),
        P(frames, packs),
    )
    return jax.shard_map(
        block,
        mesh=fine,
        in_specs=placed,
        out_specs=(P(packs, frames, None), P(frames, packs)),
        check_vma=False,
    )
```

```python
import functools
import math

import jax
import jax.numpy as jnp
from jax import lax
from jax.experimental import pallas as pl
from jax.experimental.pallas import tpu as pltpu
from jax.sharding import Mesh, PartitionSpec as P

D = 2048
HEAD_DIM = 64
TOP_K = 8
UTTS = 12
LANES = 128
TOKENS = 128
ROW = 512
WIDTH = 512
CHUNK = 256
PAIRS = WIDTH // LANES
LOCAL_LIMIT = 58
ROWS_LIMIT = 24
PACK_LIMIT = 61
PACKED = 32

ema_decay = 0.9
norm_epsilon = 1e-05
masked_score = -1e30


def pack_kernel(place_ref, teacher_ref, student_ref, qkv_hbm, *rest):
    targets, (new_ref, copies_ref), (qkv, outs, sems) = rest[:4], rest[4:6], rest[6:]

    def fetch(step):
        span = pl.ds(pl.multiple_of(step * PACKED, PACKED), PACKED)
        return pltpu.make_async_copy(qkv_hbm.at[span], qkv.at[step], sems.at[4, step])

    def deliver(step, turn):
        span = pl.ds(pl.multiple_of(step * PACKED, PACKED), PACKED)
        return pltpu.make_async_copy(
            outs.at[turn, span], targets[turn].at[span], sems.at[turn, step]
        )

    for step in range(TOKENS // PACKED):
        fetch(step).start()
    teacher_new = (
        ema_decay * teacher_ref[...].astype(jnp.float32)
        + (1.0 - ema_decay) * student_ref[...].astype(jnp.float32)
    ).astype(jnp.bfloat16)
    new_ref[...] = teacher_new
    for i in range(copies_ref.shape[0]):
        copies_ref[i] = teacher_new
    y = place_ref[1]
    low = lax.broadcasted_iota(jnp.int32, (PACKED, LANES), 1) < HEAD_DIM

    def pack(step, carry):
        fetch(step).wait()
        rows = pl.ds(pl.multiple_of(step * PACKED, PACKED), PACKED)
        for turn in range(4):
            target = lax.rem(y + 4 - turn, 4)
            odd = lax.rem(target, 2) == 1
            half = lax.div(target, 2) * LANES
            for part in range(3):
                for pair in range(PAIRS):
                    base = part * D + pair * 512
                    here = pl.ds(pl.multiple_of(base + half, LANES), LANES)
                    there = pl.ds(pl.multiple_of(base + 256 + half, LANES), LANES)
                    first = qkv[step, :, here].astype(jnp.float32)
                    second = qkv[step, :, there].astype(jnp.float32)
                    left = jnp.where(odd, pltpu.roll(first, HEAD_DIM, 1), first)
                    right = jnp.where(odd, second, pltpu.roll(second, HEAD_DIM, 1))
                    both = jnp.where(low, left, right)
                    if part == 0:
                        both = both * (1.0 / math.sqrt(HEAD_DIM))
                    start = part * WIDTH + pair * LANES
                    outs[turn, rows, start : start + LANES] = both.astype(jnp.bfloat16)
            deliver(step, turn).start()
        return carry

    lax.fori_loop(0, TOKENS // PACKED, pack, 0)
    for step in range(TOKENS // PACKED):
        for turn in range(4):
            deliver(step, turn).wait()


class Attention:
    def __init__(self, lengths_ref, place_ref):
        self.row_start = place_ref[0] * ROW
        self.y = place_ref[1]
        self.base = self.row_start - ROW
        self.ends = []
        total = jnp.int32(0)
        for j in range(UTTS):
            total = total + lengths_ref[0, j]
            self.ends.append(total)
        self.low = lax.broadcasted_iota(jnp.int32, (TOKENS, LANES), 1) < HEAD_DIM
        self.middle = lax.broadcasted_iota(jnp.int32, (2 * TOKENS, LANES), 1) == HEAD_DIM

    def steps_of(self, which):
        first = self.row_start + which * TOKENS
        last = first + TOKENS - 1
        begin = jnp.int32(0)
        finish = jnp.int32(0)
        for end in reversed(self.ends):
            finish = jnp.where(end > last, end, finish)
        for end in self.ends:
            begin = jnp.where(end <= first, end, begin)
        return lax.div(begin - self.base, CHUNK), lax.div(finish - self.base + CHUNK - 1, CHUNK)

    def segments(self, frames):
        found = jnp.zeros(frames.shape, jnp.int32)
        for end in self.ends:
            found = found + (frames >= end).astype(jnp.int32)
        return jnp.where(frames < 0, -1, found)

    def attend(self, which, queries, kv, step_of, count, scores, state, prior=None):
        low = self.low
        tops, totals, sums = (state.at[pl.ds(PAIRS * i, PAIRS)] for i in range(3))
        row_segment = self.segments(
            self.row_start + which * TOKENS + lax.broadcasted_iota(jnp.int32, (TOKENS, LANES), 0)
        )
        row_segment = jnp.concatenate([row_segment, row_segment], axis=1)
        stacked = []
        for pair in range(PAIRS):
            one = queries[pair]
            zero = jnp.zeros_like(one)
            stacked.append(
                jnp.concatenate([jnp.where(low, one, zero), jnp.where(low, zero, one)], axis=0)
            )
        tops[...] = jnp.full(tops.shape, masked_score, jnp.float32)

        def score(turn, carry):
            step, place = step_of(turn)
            start = pl.multiple_of(place * CHUNK, CHUNK)
            key_segment = self.segments(
                self.base + step * CHUNK + lax.broadcasted_iota(jnp.int32, (8, CHUNK), 1)
            )[:1]
            allowed = row_segment == key_segment
            allowed = jnp.concatenate([allowed, allowed], axis=0)
            for pair in range(PAIRS):
                keys = kv[pl.ds(start, CHUNK), pair * LANES : (pair + 1) * LANES]
                found = lax.dot_general(
                    stacked[pair], keys, (((1,), (1,)), ((), ())),
                    preferred_element_type=jnp.float32,
                )
                found = jnp.where(allowed, found, masked_score)
                scores[turn, pair] = found
                tops[pair] = jnp.maximum(
                    tops[pair], jnp.maximum(found[:, :LANES], found[:, LANES:])
                )
            return carry

        lax.fori_loop(0, count, score, 0)
        for pair in range(PAIRS):
            top = jnp.max(tops[pair], axis=1, keepdims=True)
            top = jnp.broadcast_to(top, (2 * TOKENS, LANES))
            if prior is None:
                tops[pair] = top
                totals[pair] = jnp.zeros((2 * TOKENS, LANES), jnp.float32)
                sums[pair] = jnp.zeros((2 * TOKENS, LANES), jnp.float32)
            else:
                stats = jnp.concatenate([prior[2 * pair], prior[2 * pair + 1]], axis=0)
                old = jnp.broadcast_to(stats[:, :1], (2 * TOKENS, LANES))
                top = jnp.maximum(top, old)
                tops[pair] = top
                factor = jnp.exp(old - top)
                totals[pair] = jnp.where(self.middle, stats * factor, 0.0)
                known = prior[2 * PAIRS + pair]
                sums[pair] = jnp.concatenate([known, known], axis=0) * factor

        def mix(turn, carry):
            _, place = step_of(turn)
            start = pl.multiple_of(place * CHUNK, CHUNK)
            for pair in range(PAIRS):
                found = scores[turn, pair]
                left = jnp.exp(found[:, :LANES] - tops[pair])
                right = jnp.exp(found[:, LANES:] - tops[pair])
                totals[pair] = totals[pair] + (left + right)
                weights = jnp.concatenate([left, right], axis=1).astype(jnp.bfloat16)
                values = kv[
                    pl.ds(start, CHUNK), WIDTH + pair * LANES : WIDTH + (pair + 1) * LANES
                ]
                sums[pair] = sums[pair] + jnp.dot(
                    weights, values, preferred_element_type=jnp.float32
                )
            return carry

        lax.fori_loop(0, count, mix, 0)


def local_kernel(lengths_ref, place_ref, own, next_piece, far, last, *rest):
    outs, (kv, queries, scores, state, packed, sems) = rest[:4], rest[4:]
    attention = Attention(lengths_ref, place_ref)
    pieces = (own, next_piece, far, last)
    asks, copies = [], []
    for turn in range(4):
        slot = lax.rem(attention.y + turn, 4)
        asks.append(
            pltpu.make_async_copy(
                pieces[turn].at[:, pl.ds(0, WIDTH)], queries.at[turn], sems.at[4 + turn]
            )
        )
        copies.append(
            pltpu.make_async_copy(
                pieces[turn].at[:, pl.ds(WIDTH, 2 * WIDTH)],
                kv.at[pl.ds(pl.multiple_of(slot * TOKENS, TOKENS), TOKENS)],
                sems.at[turn],
            )
        )
    for copy in asks + copies:
        copy.start()
    for copy in asks + copies:
        copy.wait()
    stores = []
    for i, offset in enumerate((2, 1, 3, 0)):
        which = lax.rem(attention.y + offset, 4)
        start, stop = attention.steps_of(which)
        start, stop = jnp.maximum(start, 2), jnp.minimum(stop, 4)
        asked = [queries[offset, :, pair * LANES : (pair + 1) * LANES] for pair in range(PAIRS)]
        attention.attend(
            which, asked, kv,
            lambda turn: (start + turn, start + turn - 2), stop - start,
            scores, state,
        )
        if i >= 2:
            stores[i - 2].wait()
        tiles = packed.at[i % 2]
        for pair in range(PAIRS):
            total = jnp.sum(state[PAIRS + pair], axis=1, keepdims=True)
            total = jnp.broadcast_to(total, (2 * TOKENS, LANES))
            top, found = state[pair], state[2 * PAIRS + pair]
            tiles[2 * pair] = jnp.where(attention.low, top[:TOKENS], total[:TOKENS])
            tiles[2 * pair + 1] = jnp.where(attention.low, top[TOKENS:], total[TOKENS:])
            tiles[2 * PAIRS + pair] = jnp.where(attention.low, found[:TOKENS], found[TOKENS:])
            tiles[3 * PAIRS + pair] = asked[pair].astype(jnp.float32)
        stores.append(pltpu.make_async_copy(tiles, outs[offset], sems.at[8 + i]))
        stores[i].start()
    stores[2].wait()
    stores[3].wait()


def project(mixed, core, own_weights, other_weights, store):
    for tile in range(8):
        high, place = divmod(tile, 4)
        both = jnp.concatenate([own_weights[place, high], other_weights[place, high]], axis=1)
        found = jnp.dot(mixed, both, preferred_element_type=jnp.float32)
        start = tile * 2 * LANES
        store(tile, pl.multiple_of(start + core * LANES, LANES), found[:, :LANES])
        store(tile, pl.multiple_of(start + (1 - core) * LANES, LANES), found[:, LANES:])


def attend_rows(offsets, lengths_ref, place_ref, before, after, priors, kv, scores, state, mixed, sems):
    attention = Attention(lengths_ref, place_ref)
    whiches, aheads, behinds = [], [], []
    for offset in offsets:
        which = lax.rem(attention.y + offset, 4)
        start, stop = attention.steps_of(which)
        whiches.append(which)
        aheads.append(jnp.maximum(2 - start, 0))
        behinds.append(jnp.maximum(stop - 4, 0))
    most_ahead = functools.reduce(jnp.maximum, aheads)
    most_behind = functools.reduce(jnp.maximum, behinds)
    copies = []
    for side, source in enumerate((before, after)):
        for turn in range(4):
            slot = lax.rem(attention.y + turn, 4)
            half = lax.div(slot, 2)
            copy = pltpu.make_async_copy(
                source.at[pl.ds(turn * TOKENS, TOKENS)],
                kv.at[pl.ds(pl.multiple_of((4 * side + slot) * TOKENS, TOKENS), TOKENS)],
                sems.at[4 * side + turn],
            )
            copies.append((half < most_behind if side else half >= 2 - most_ahead, copy))
    for wanted, copy in copies:
        @pl.when(wanted)
        def _():
            copy.start()
    for wanted, copy in copies:
        @pl.when(wanted)
        def _():
            copy.wait()
    for i, which in enumerate(whiches):
        ahead, behind, prior = aheads[i], behinds[i], priors[i]

        def step_of(turn):
            early = turn < ahead
            step = jnp.where(early, 2 - ahead + turn, 4 + turn - ahead)
            return step, jnp.where(early, step, step - 2)

        queries = [prior[3 * PAIRS + pair].astype(jnp.bfloat16) for pair in range(PAIRS)]
        attention.attend(which, queries, kv, step_of, ahead + behind, scores, state, prior)
        for pair in range(PAIRS):
            row_total = jnp.sum(state[PAIRS + pair], axis=1, keepdims=True)
            found = state[2 * PAIRS + pair] / row_total
            mixed[i * TOKENS : (i + 1) * TOKENS, pair * LANES : (pair + 1) * LANES] = jnp.where(
                attention.low, found[:TOKENS], found[TOKENS:]
            ).astype(jnp.bfloat16)


def attend_kernel(offsets, lengths_ref, place_ref, before, after, *rest):
    count = len(offsets)
    priors, (mixed, *scratch) = rest[:count], rest[count:]
    kv, scores, state, sems = scratch
    attend_rows(
        offsets, lengths_ref, place_ref, before, after, priors, kv, scores, state, mixed, sems
    )


HALF = D // 2


def project_kernel(place_ref, own_weights, other_weights, mixed, first_ref, second_ref):
    def store(tile, start, value):
        out_ref = first_ref if tile < 4 else second_ref
        start = pl.multiple_of(start - tile // 4 * HALF, LANES)
        out_ref[:, pl.ds(start, LANES)] = value.astype(out_ref.dtype)

    project(mixed[...], place_ref[2], own_weights, other_weights, store)


def rows_kernel(
    offset, lengths_ref, place_ref, own_weights, other_weights, before, after, prior, *rest
):
    passed, (out_ref, kv, scores, state, sems, mixed) = rest[:-6], rest[-6:]
    attend_rows(
        (offset,), lengths_ref, place_ref, before, after, (prior,), kv, scores, state, mixed, sems
    )

    def store(tile, start, value):
        if passed and tile >= 4:
            more = passed[0][:, pl.ds(pl.multiple_of(start - HALF, LANES), LANES)]
            value = value + more.astype(jnp.float32)
        out_ref[:, pl.ds(start, LANES)] = value.astype(out_ref.dtype)

    project(mixed[...], place_ref[2], own_weights, other_weights, store)


def finish_kernel(own_ref, one_ref, two_ref, three_ref, resid_ref, earlier_ref, out_ref):
    far = one_ref[...].astype(jnp.float32)
    branch = own_ref[...] + jnp.concatenate([far, jnp.zeros_like(far)], axis=1)
    branch = branch + two_ref[...].astype(jnp.float32)
    branch = branch + three_ref[...].astype(jnp.float32)
    summed = resid_ref[...].astype(jnp.float32) + branch * (1.0 / math.sqrt(D))
    centered = summed - jnp.mean(summed, axis=1, keepdims=True)
    spread = jnp.mean(centered * centered, axis=1, keepdims=True)
    normed = centered * lax.rsqrt(spread + norm_epsilon)
    out_ref[...] = (earlier_ref[...] + normed) * (1.0 / TOP_K)


vmem = pl.BlockSpec(memory_space=pltpu.VMEM)
smem = pl.BlockSpec(memory_space=pltpu.SMEM)
anywhere = pl.BlockSpec(memory_space=pl.ANY)
running = (3 * PAIRS, 2 * TOKENS, LANES)
handed = (4 * PAIRS, TOKENS, LANES)
local_scratch = [
    pltpu.VMEM((ROW, 2 * WIDTH), jnp.bfloat16),
    pltpu.VMEM((4, TOKENS, WIDTH), jnp.bfloat16),
    pltpu.VMEM((2, PAIRS, 2 * TOKENS, CHUNK), jnp.float32),
    pltpu.VMEM(running, jnp.float32),
    pltpu.VMEM((2,) + handed, jnp.float32),
    pltpu.SemaphoreType.DMA((12,)),
]
rows_scratch = [
    pltpu.VMEM((2 * ROW, 2 * WIDTH), jnp.bfloat16),
    pltpu.VMEM((4, PAIRS, 2 * TOKENS, CHUNK), jnp.float32),
    pltpu.VMEM(running, jnp.float32),
    pltpu.SemaphoreType.DMA((8,)),
]


def cost(flops, moved, exps=0):
    return pl.CostEstimate(flops=flops, bytes_accessed=moved, transcendentals=exps)


def limit(mebibytes):
    return pltpu.CompilerParams(vmem_limit_bytes=mebibytes << 20)


def array(*shape, dtype=jnp.bfloat16):
    return jax.ShapeDtypeStruct(shape, dtype)


def shift(value, amount, axis="y", size=4):
    return lax.ppermute(value, axis, [(i, (i + amount) % size) for i in range(size)])


def block(qkv, resid, earlier, lengths, teacher_out, student_out):
    place = jnp.stack([lax.axis_index(name) for name in ("z", "y", "c")]).astype(jnp.int32)
    ring = 2 * lax.axis_size("z")
    pack = pl.pallas_call(
        pack_kernel,
        out_shape=(array(TOKENS, 3 * WIDTH),) * 4
        + (array(*teacher_out.shape), array(ring, *teacher_out.shape)),
        in_specs=[smem, vmem, vmem, anywhere],
        out_specs=(anywhere,) * 4 + (vmem,) * 2,
        scratch_shapes=[
            pltpu.VMEM((TOKENS // PACKED, PACKED, 3 * D), jnp.bfloat16),
            pltpu.VMEM((4, TOKENS, 3 * WIDTH), jnp.bfloat16),
            pltpu.SemaphoreType.DMA((5, TOKENS // PACKED)),
        ],
        compiler_params=limit(PACK_LIMIT),
        cost_estimate=cost(0, 3 << 20),
        name="pack",
    )
    *packed, teacher_new, copies = pack(place, teacher_out, student_out, qkv[0])

    pieces = [packed[0]]
    for turn in (1, 2, 3):
        pieces.append(shift(packed[turn], -turn))
    keys = jnp.concatenate([piece[:, WIDTH:] for piece in pieces], axis=0)
    after = shift(keys, -1, ("h", "z"), ring)
    before = shift(keys, 1, ("h", "z"), ring)

    ring_weights = lax.all_to_all(copies, ("h", "z"), 0, 0, tiled=True)
    ring_weights = ring_weights.reshape(2, ROW, LANES)
    own_weights = lax.all_to_all(
        jnp.broadcast_to(ring_weights[None], (4,) + ring_weights.shape), "x", 0, 0, tiled=True
    )
    other_weights = shift(own_weights, 1, "c", 2)

    local = pl.pallas_call(
        local_kernel,
        out_shape=(array(*handed, dtype=jnp.float32),) * 4,
        in_specs=[smem, smem] + [anywhere] * 4,
        out_specs=(anywhere,) * 4,
        scratch_shapes=local_scratch,
        compiler_params=limit(LOCAL_LIMIT),
        cost_estimate=cost(1 << 30, 8 << 20, 2 << 20),
        name="local",
    )(lengths, place, *pieces)

    def rows_of(offset, dtype, *passed):
        return pl.pallas_call(
            functools.partial(rows_kernel, offset),
            out_shape=array(TOKENS, D, dtype=dtype),
            in_specs=[smem, smem, vmem, vmem, anywhere, anywhere, vmem] + [vmem] * len(passed),
            out_specs=vmem,
            scratch_shapes=rows_scratch + [pltpu.VMEM((TOKENS, WIDTH), jnp.bfloat16)],
            compiler_params=limit(ROWS_LIMIT),
            cost_estimate=cost(1 << 29, 4 << 20, 1 << 20),
            name="rows",
        )(lengths, place, own_weights, other_weights, before, after, local[offset], *passed)

    mixed = pl.pallas_call(
        functools.partial(attend_kernel, (2,)),
        out_shape=array(TOKENS, WIDTH),
        in_specs=[smem, smem, anywhere, anywhere, vmem],
        out_specs=vmem,
        scratch_shapes=rows_scratch,
        compiler_params=limit(ROWS_LIMIT),
        cost_estimate=cost(1 << 28, 3 << 20, 1 << 20),
        name="attend",
    )(lengths, place, before, after, local[2])
    far, passed = pl.pallas_call(
        project_kernel,
        out_shape=(array(TOKENS, HALF),) * 2,
        in_specs=[smem, vmem, vmem, vmem],
        out_specs=(vmem,) * 2,
        compiler_params=limit(8),
        cost_estimate=cost(2 * TOKENS * WIDTH * D, 3 << 20),
        name="project",
    )(place, own_weights, other_weights, mixed)
    passed = shift(passed, 3)
    far = shift(far, 2)
    up = rows_of(1, jnp.bfloat16)
    up = shift(up, 1)
    down = rows_of(3, jnp.bfloat16, passed)
    down = shift(down, 3)
    own = rows_of(0, jnp.float32)
    rows = pl.BlockSpec((32, D), lambda i: (i, 0))
    targets = pl.pallas_call(
        finish_kernel,
        grid=(4,),
        out_shape=array(TOKENS, D, dtype=jnp.float32),
        in_specs=[rows, pl.BlockSpec((32, HALF), lambda i: (i, 0))] + [rows] * 4,
        out_specs=rows,
        compiler_params=limit(12),
        cost_estimate=cost(1 << 22, 5 << 20),
        name="finish",
    )(own, far, up, down, resid[0], earlier[0])
    return (targets[None], teacher_new)


def solution(mesh):
    fine = Mesh(
        mesh.devices.reshape(2, 4, 2, 8, 4), ("h", "x", "c", "z", "y")
    )
    packs, frames = ("h", "x", "c"), ("z", "y")
    placed = (
        P(packs, frames, None),
        P(packs, frames, None),
        P(packs, frames, None),
        P(packs, None),
        P(frames, packs),
        P(frames, packs),
    )
    return jax.shard_map(
        block,
        mesh=fine,
        in_specs=placed,
        out_specs=(P(packs, frames, None), P(frames, packs)),
        check_vma=False,
    )
```

```python
import functools
import math

import jax
import jax.numpy as jnp
from jax import lax
from jax.experimental import pallas as pl
from jax.experimental.pallas import tpu as pltpu
from jax.sharding import Mesh, PartitionSpec as P

D = 2048
HEAD_DIM = 64
TOP_K = 8
UTTS = 12
LANES = 128
TOKENS = 128
ROW = 512
WIDTH = 512
CHUNK = 256
PAIRS = WIDTH // LANES
LOCAL_LIMIT = 58
ROWS_LIMIT = 24
PACKED = 32

ema_decay = 0.9
norm_epsilon = 1e-05
masked_score = -1e30


def pack_kernel(place_ref, qkv_ref, *outs):
    y = place_ref[1]
    low = lax.broadcasted_iota(jnp.int32, (PACKED, LANES), 1) < HEAD_DIM
    for turn in range(4):
        target = lax.rem(y + 4 - turn, 4)
        odd = lax.rem(target, 2) == 1
        half = lax.div(target, 2) * LANES
        for part in range(3):
            for pair in range(PAIRS):
                base = part * D + pair * 512
                first = qkv_ref[:, pl.ds(pl.multiple_of(base + half, LANES), LANES)].astype(jnp.float32)
                second = qkv_ref[:, pl.ds(pl.multiple_of(base + 256 + half, LANES), LANES)].astype(jnp.float32)
                left = jnp.where(odd, pltpu.roll(first, HEAD_DIM, 1), first)
                right = jnp.where(odd, second, pltpu.roll(second, HEAD_DIM, 1))
                both = jnp.where(low, left, right)
                if part == 0:
                    both = both * (1.0 / math.sqrt(HEAD_DIM))
                start = part * WIDTH + pair * LANES
                outs[turn][:, start : start + LANES] = both.astype(jnp.bfloat16)


class Attention:
    def __init__(self, lengths_ref, place_ref):
        self.row_start = place_ref[0] * ROW
        self.y = place_ref[1]
        self.base = self.row_start - ROW
        self.ends = []
        total = jnp.int32(0)
        for j in range(UTTS):
            total = total + lengths_ref[0, j]
            self.ends.append(total)
        self.low = lax.broadcasted_iota(jnp.int32, (TOKENS, LANES), 1) < HEAD_DIM
        self.middle = lax.broadcasted_iota(jnp.int32, (2 * TOKENS, LANES), 1) == HEAD_DIM

    def steps_of(self, which):
        first = self.row_start + which * TOKENS
        last = first + TOKENS - 1
        begin = jnp.int32(0)
        finish = jnp.int32(0)
        for end in reversed(self.ends):
            finish = jnp.where(end > last, end, finish)
        for end in self.ends:
            begin = jnp.where(end <= first, end, begin)
        return lax.div(begin - self.base, CHUNK), lax.div(finish - self.base + CHUNK - 1, CHUNK)

    def segments(self, frames):
        found = jnp.zeros(frames.shape, jnp.int32)
        for end in self.ends:
            found = found + (frames >= end).astype(jnp.int32)
        return jnp.where(frames < 0, -1, found)

    def attend(self, which, queries, kv, step_of, count, scores, state, prior=None):
        low = self.low
        tops, totals, sums = (state.at[pl.ds(PAIRS * i, PAIRS)] for i in range(3))
        row_segment = self.segments(
            self.row_start + which * TOKENS + lax.broadcasted_iota(jnp.int32, (TOKENS, LANES), 0)
        )
        row_segment = jnp.concatenate([row_segment, row_segment], axis=1)
        stacked = []
        for pair in range(PAIRS):
            one = queries[pair]
            zero = jnp.zeros_like(one)
            stacked.append(
                jnp.concatenate([jnp.where(low, one, zero), jnp.where(low, zero, one)], axis=0)
            )
        tops[...] = jnp.full(tops.shape, masked_score, jnp.float32)

        def score(turn, carry):
            step, place = step_of(turn)
            start = pl.multiple_of(place * CHUNK, CHUNK)
            key_segment = self.segments(
                self.base + step * CHUNK + lax.broadcasted_iota(jnp.int32, (8, CHUNK), 1)
            )[:1]
            allowed = row_segment == key_segment
            allowed = jnp.concatenate([allowed, allowed], axis=0)
            for pair in range(PAIRS):
                keys = kv[pl.ds(start, CHUNK), pair * LANES : (pair + 1) * LANES]
                found = lax.dot_general(
                    stacked[pair], keys, (((1,), (1,)), ((), ())),
                    preferred_element_type=jnp.float32,
                )
                found = jnp.where(allowed, found, masked_score)
                scores[turn, pair] = found
                tops[pair] = jnp.maximum(
                    tops[pair], jnp.maximum(found[:, :LANES], found[:, LANES:])
                )
            return carry

        lax.fori_loop(0, count, score, 0)
        for pair in range(PAIRS):
            top = jnp.max(tops[pair], axis=1, keepdims=True)
            top = jnp.broadcast_to(top, (2 * TOKENS, LANES))
            if prior is None:
                tops[pair] = top
                totals[pair] = jnp.zeros((2 * TOKENS, LANES), jnp.float32)
                sums[pair] = jnp.zeros((2 * TOKENS, LANES), jnp.float32)
            else:
                stats = jnp.concatenate([prior[2 * pair], prior[2 * pair + 1]], axis=0)
                old = jnp.broadcast_to(stats[:, :1], (2 * TOKENS, LANES))
                top = jnp.maximum(top, old)
                tops[pair] = top
                factor = jnp.exp(old - top)
                totals[pair] = jnp.where(self.middle, stats * factor, 0.0)
                known = prior[2 * PAIRS + pair]
                sums[pair] = jnp.concatenate([known, known], axis=0) * factor

        def mix(turn, carry):
            _, place = step_of(turn)
            start = pl.multiple_of(place * CHUNK, CHUNK)
            for pair in range(PAIRS):
                found = scores[turn, pair]
                left = jnp.exp(found[:, :LANES] - tops[pair])
                right = jnp.exp(found[:, LANES:] - tops[pair])
                totals[pair] = totals[pair] + (left + right)
                weights = jnp.concatenate([left, right], axis=1).astype(jnp.bfloat16)
                values = kv[
                    pl.ds(start, CHUNK), WIDTH + pair * LANES : WIDTH + (pair + 1) * LANES
                ]
                sums[pair] = sums[pair] + jnp.dot(
                    weights, values, preferred_element_type=jnp.float32
                )
            return carry

        lax.fori_loop(0, count, mix, 0)


def local_kernel(lengths_ref, place_ref, own, next_piece, far, last, *rest):
    outs, (kv, queries, scores, state, packed, sems) = rest[:4], rest[4:]
    attention = Attention(lengths_ref, place_ref)
    pieces = (own, next_piece, far, last)
    asks, copies = [], []
    for turn in range(4):
        slot = lax.rem(attention.y + turn, 4)
        asks.append(
            pltpu.make_async_copy(
                pieces[turn].at[:, pl.ds(0, WIDTH)], queries.at[turn], sems.at[4 + turn]
            )
        )
        copies.append(
            pltpu.make_async_copy(
                pieces[turn].at[:, pl.ds(WIDTH, 2 * WIDTH)],
                kv.at[pl.ds(pl.multiple_of(slot * TOKENS, TOKENS), TOKENS)],
                sems.at[turn],
            )
        )
    for copy in asks + copies:
        copy.start()
    for copy in asks + copies:
        copy.wait()
    stores = []
    for i, offset in enumerate((2, 1, 3, 0)):
        which = lax.rem(attention.y + offset, 4)
        start, stop = attention.steps_of(which)
        start, stop = jnp.maximum(start, 2), jnp.minimum(stop, 4)
        asked = [queries[offset, :, pair * LANES : (pair + 1) * LANES] for pair in range(PAIRS)]
        attention.attend(
            which, asked, kv,
            lambda turn: (start + turn, start + turn - 2), stop - start,
            scores, state,
        )
        if i >= 2:
            stores[i - 2].wait()
        tiles = packed.at[i % 2]
        for pair in range(PAIRS):
            total = jnp.sum(state[PAIRS + pair], axis=1, keepdims=True)
            total = jnp.broadcast_to(total, (2 * TOKENS, LANES))
            top, found = state[pair], state[2 * PAIRS + pair]
            tiles[2 * pair] = jnp.where(attention.low, top[:TOKENS], total[:TOKENS])
            tiles[2 * pair + 1] = jnp.where(attention.low, top[TOKENS:], total[TOKENS:])
            tiles[2 * PAIRS + pair] = jnp.where(attention.low, found[:TOKENS], found[TOKENS:])
            tiles[3 * PAIRS + pair] = asked[pair].astype(jnp.float32)
        stores.append(pltpu.make_async_copy(tiles, outs[offset], sems.at[8 + i]))
        stores[i].start()
    stores[2].wait()
    stores[3].wait()


def project(mixed, core, own_weights, other_weights, store):
    for tile in range(8):
        high, place = divmod(tile, 4)
        both = jnp.concatenate([own_weights[place, high], other_weights[place, high]], axis=1)
        found = jnp.dot(mixed, both, preferred_element_type=jnp.float32)
        start = tile * 2 * LANES
        store(tile, pl.multiple_of(start + core * LANES, LANES), found[:, :LANES])
        store(tile, pl.multiple_of(start + (1 - core) * LANES, LANES), found[:, LANES:])


def attend_rows(offsets, lengths_ref, place_ref, before, after, priors, kv, scores, state, mixed, sems):
    attention = Attention(lengths_ref, place_ref)
    whiches, aheads, behinds = [], [], []
    for offset in offsets:
        which = lax.rem(attention.y + offset, 4)
        start, stop = attention.steps_of(which)
        whiches.append(which)
        aheads.append(jnp.maximum(2 - start, 0))
        behinds.append(jnp.maximum(stop - 4, 0))
    most_ahead = functools.reduce(jnp.maximum, aheads)
    most_behind = functools.reduce(jnp.maximum, behinds)
    copies = []
    for side, source in enumerate((before, after)):
        for turn in range(4):
            slot = lax.rem(attention.y + turn, 4)
            half = lax.div(slot, 2)
            copy = pltpu.make_async_copy(
                source.at[pl.ds(turn * TOKENS, TOKENS)],
                kv.at[pl.ds(pl.multiple_of((4 * side + slot) * TOKENS, TOKENS), TOKENS)],
                sems.at[4 * side + turn],
            )
            copies.append((half < most_behind if side else half >= 2 - most_ahead, copy))
    for wanted, copy in copies:
        @pl.when(wanted)
        def _():
            copy.start()
    for wanted, copy in copies:
        @pl.when(wanted)
        def _():
            copy.wait()
    for i, which in enumerate(whiches):
        ahead, behind, prior = aheads[i], behinds[i], priors[i]

        def step_of(turn):
            early = turn < ahead
            step = jnp.where(early, 2 - ahead + turn, 4 + turn - ahead)
            return step, jnp.where(early, step, step - 2)

        queries = [prior[3 * PAIRS + pair].astype(jnp.bfloat16) for pair in range(PAIRS)]
        attention.attend(which, queries, kv, step_of, ahead + behind, scores, state, prior)
        for pair in range(PAIRS):
            row_total = jnp.sum(state[PAIRS + pair], axis=1, keepdims=True)
            found = state[2 * PAIRS + pair] / row_total
            mixed[i * TOKENS : (i + 1) * TOKENS, pair * LANES : (pair + 1) * LANES] = jnp.where(
                attention.low, found[:TOKENS], found[TOKENS:]
            ).astype(jnp.bfloat16)


def attend_kernel(offsets, lengths_ref, place_ref, before, after, *rest):
    count = len(offsets)
    priors, (mixed, *scratch) = rest[:count], rest[count:]
    kv, scores, state, sems = scratch
    attend_rows(
        offsets, lengths_ref, place_ref, before, after, priors, kv, scores, state, mixed, sems
    )


HALF = D // 2


def project_kernel(place_ref, own_weights, other_weights, mixed, first_ref, second_ref):
    def store(tile, start, value):
        out_ref = first_ref if tile < 4 else second_ref
        start = pl.multiple_of(start - tile // 4 * HALF, LANES)
        out_ref[:, pl.ds(start, LANES)] = value.astype(out_ref.dtype)

    project(mixed[...], place_ref[2], own_weights, other_weights, store)


def rows_kernel(
    offset, lengths_ref, place_ref, own_weights, other_weights, before, after, prior, *rest
):
    passed, (out_ref, kv, scores, state, sems, mixed) = rest[:-6], rest[-6:]
    attend_rows(
        (offset,), lengths_ref, place_ref, before, after, (prior,), kv, scores, state, mixed, sems
    )

    def store(tile, start, value):
        if passed and tile >= 4:
            more = passed[0][:, pl.ds(pl.multiple_of(start - HALF, LANES), LANES)]
            value = value + more.astype(jnp.float32)
        out_ref[:, pl.ds(start, LANES)] = value.astype(out_ref.dtype)

    project(mixed[...], place_ref[2], own_weights, other_weights, store)


def finish_kernel(own_ref, far_ref, up_ref, down_ref, resid_ref, earlier_ref, out_hbm, out, sems):
    def deliver(step):
        rows = pl.ds(pl.multiple_of(step * PACKED, PACKED), PACKED)
        return pltpu.make_async_copy(out.at[rows], out_hbm.at[rows], sems.at[step])

    def finish(step, carry):
        rows = pl.ds(pl.multiple_of(step * PACKED, PACKED), PACKED)
        far = far_ref[rows].astype(jnp.float32)
        branch = own_ref[rows] + jnp.concatenate([far, jnp.zeros_like(far)], axis=1)
        branch = branch + up_ref[rows].astype(jnp.float32)
        branch = branch + down_ref[rows].astype(jnp.float32)
        summed = resid_ref[rows].astype(jnp.float32) + branch * (1.0 / math.sqrt(D))
        centered = summed - jnp.mean(summed, axis=1, keepdims=True)
        spread = jnp.mean(centered * centered, axis=1, keepdims=True)
        normed = centered * lax.rsqrt(spread + norm_epsilon)
        out[rows] = (earlier_ref[rows] + normed) * (1.0 / TOP_K)
        deliver(step).start()
        return carry

    steps = TOKENS // PACKED
    lax.fori_loop(0, steps, finish, 0)
    for step in range(steps):
        deliver(step).wait()


vmem = pl.BlockSpec(memory_space=pltpu.VMEM)
smem = pl.BlockSpec(memory_space=pltpu.SMEM)
anywhere = pl.BlockSpec(memory_space=pl.ANY)
running = (3 * PAIRS, 2 * TOKENS, LANES)
handed = (4 * PAIRS, TOKENS, LANES)
local_scratch = [
    pltpu.VMEM((ROW, 2 * WIDTH), jnp.bfloat16),
    pltpu.VMEM((4, TOKENS, WIDTH), jnp.bfloat16),
    pltpu.VMEM((2, PAIRS, 2 * TOKENS, CHUNK), jnp.float32),
    pltpu.VMEM(running, jnp.float32),
    pltpu.VMEM((2,) + handed, jnp.float32),
    pltpu.SemaphoreType.DMA((12,)),
]
rows_scratch = [
    pltpu.VMEM((2 * ROW, 2 * WIDTH), jnp.bfloat16),
    pltpu.VMEM((4, PAIRS, 2 * TOKENS, CHUNK), jnp.float32),
    pltpu.VMEM(running, jnp.float32),
    pltpu.SemaphoreType.DMA((8,)),
]


def cost(flops, moved, exps=0):
    return pl.CostEstimate(flops=flops, bytes_accessed=moved, transcendentals=exps)


def limit(mebibytes):
    return pltpu.CompilerParams(vmem_limit_bytes=mebibytes << 20)


def array(*shape, dtype=jnp.bfloat16):
    return jax.ShapeDtypeStruct(shape, dtype)


def shift(value, amount, axis="y", size=4):
    return lax.ppermute(value, axis, [(i, (i + amount) % size) for i in range(size)])


def block(qkv, resid, earlier, lengths, teacher_out, student_out):
    teacher_new = (
        ema_decay * teacher_out.astype(jnp.float32)
        + (1.0 - ema_decay) * student_out.astype(jnp.float32)
    ).astype(jnp.bfloat16)
    place = jnp.stack([lax.axis_index(name) for name in ("z", "y", "c")]).astype(jnp.int32)

    pack = pl.pallas_call(
        pack_kernel,
        grid=(TOKENS // PACKED,),
        out_shape=(array(TOKENS, 3 * WIDTH),) * 4,
        in_specs=[smem, pl.BlockSpec((PACKED, 3 * D), lambda i: (i, 0))],
        out_specs=(pl.BlockSpec((PACKED, 3 * WIDTH), lambda i: (i, 0)),) * 4,
        compiler_params=limit(12),
        cost_estimate=cost(0, 3 << 20),
        name="pack",
    )
    packed = pack(place, qkv[0])

    pieces = [packed[0]]
    for turn in (1, 2, 3):
        pieces.append(shift(packed[turn], -turn))
    ring = 2 * lax.axis_size("z")
    keys = jnp.concatenate([piece[:, WIDTH:] for piece in pieces], axis=0)
    after = shift(keys, -1, ("h", "z"), ring)
    before = shift(keys, 1, ("h", "z"), ring)

    ring_weights = lax.all_to_all(
        jnp.broadcast_to(teacher_new[None], (16,) + teacher_new.shape), ("h", "z"), 0, 0, tiled=True
    )
    ring_weights = ring_weights.reshape(2, ROW, LANES)
    own_weights = lax.all_to_all(
        jnp.broadcast_to(ring_weights[None], (4,) + ring_weights.shape), "x", 0, 0, tiled=True
    )
    other_weights = shift(own_weights, 1, "c", 2)

    local = pl.pallas_call(
        local_kernel,
        out_shape=(array(*handed, dtype=jnp.float32),) * 4,
        in_specs=[smem, smem] + [anywhere] * 4,
        out_specs=(anywhere,) * 4,
        scratch_shapes=local_scratch,
        compiler_params=limit(LOCAL_LIMIT),
        cost_estimate=cost(1 << 30, 8 << 20, 2 << 20),
        name="local",
    )(lengths, place, *pieces)

    def rows_of(offset, dtype, *passed):
        return pl.pallas_call(
            functools.partial(rows_kernel, offset),
            out_shape=array(TOKENS, D, dtype=dtype),
            in_specs=[smem, smem, vmem, vmem, anywhere, anywhere, vmem] + [vmem] * len(passed),
            out_specs=vmem,
            scratch_shapes=rows_scratch + [pltpu.VMEM((TOKENS, WIDTH), jnp.bfloat16)],
            compiler_params=limit(ROWS_LIMIT),
            cost_estimate=cost(1 << 29, 4 << 20, 1 << 20),
            name="rows",
        )(lengths, place, own_weights, other_weights, before, after, local[offset], *passed)

    mixed = pl.pallas_call(
        functools.partial(attend_kernel, (2,)),
        out_shape=array(TOKENS, WIDTH),
        in_specs=[smem, smem, anywhere, anywhere, vmem],
        out_specs=vmem,
        scratch_shapes=rows_scratch,
        compiler_params=limit(ROWS_LIMIT),
        cost_estimate=cost(1 << 28, 3 << 20, 1 << 20),
        name="attend",
    )(lengths, place, before, after, local[2])
    far, passed = pl.pallas_call(
        project_kernel,
        out_shape=(array(TOKENS, HALF),) * 2,
        in_specs=[smem, vmem, vmem, vmem],
        out_specs=(vmem,) * 2,
        compiler_params=limit(8),
        cost_estimate=cost(2 * TOKENS * WIDTH * D, 3 << 20),
        name="project",
    )(place, own_weights, other_weights, mixed)
    passed = shift(passed, 1)
    far = shift(far, 2)
    down = rows_of(3, jnp.bfloat16)
    down = shift(down, 3)
    up = rows_of(1, jnp.bfloat16, passed)
    up = shift(up, 1)
    own = rows_of(0, jnp.float32)
    targets = pl.pallas_call(
        finish_kernel,
        out_shape=array(TOKENS, D, dtype=jnp.float32),
        in_specs=[vmem] * 6,
        out_specs=anywhere,
        scratch_shapes=[
            pltpu.VMEM((TOKENS, D), jnp.float32),
            pltpu.SemaphoreType.DMA((TOKENS // PACKED,)),
        ],
        compiler_params=limit(12),
        cost_estimate=cost(1 << 22, 5 << 20),
        name="finish",
    )(own, far, up, down, resid[0], earlier[0])
    return (targets[None], teacher_new)


def solution(mesh):
    fine = Mesh(
        mesh.devices.reshape(2, 4, 2, 8, 4), ("h", "x", "c", "z", "y")
    )
    packs, frames = ("h", "x", "c"), ("z", "y")
    placed = (
        P(packs, frames, None),
        P(packs, frames, None),
        P(packs, frames, None),
        P(packs, None),
        P(frames, packs),
        P(frames, packs),
    )
    return jax.shard_map(
        block,
        mesh=fine,
        in_specs=placed,
        out_specs=(P(packs, frames, None), P(frames, packs)),
        check_vma=False,
    )
```

```python
import functools
import math

import jax
import jax.numpy as jnp
from jax import lax
from jax.experimental import pallas as pl
from jax.experimental.pallas import tpu as pltpu
from jax.sharding import Mesh, PartitionSpec as P

D = 2048
HEAD_DIM = 64
TOP_K = 8
UTTS = 12
LANES = 128
TOKENS = 128
ROW = 512
WIDTH = 512
CHUNK = 256
PAIRS = WIDTH // LANES
LOCAL_LIMIT = 58
ROWS_LIMIT = 24
PACKED = 32

ema_decay = 0.9
norm_epsilon = 1e-05
masked_score = -1e30


def pack_kernel(place_ref, qkv_ref, *outs):
    y = place_ref[1]
    low = lax.broadcasted_iota(jnp.int32, (PACKED, LANES), 1) < HEAD_DIM
    for turn in range(4):
        target = lax.rem(y + 4 - turn, 4)
        odd = lax.rem(target, 2) == 1
        half = lax.div(target, 2) * LANES
        for part in range(3):
            for pair in range(PAIRS):
                base = part * D + pair * 512
                first = qkv_ref[:, pl.ds(pl.multiple_of(base + half, LANES), LANES)].astype(jnp.float32)
                second = qkv_ref[:, pl.ds(pl.multiple_of(base + 256 + half, LANES), LANES)].astype(jnp.float32)
                left = jnp.where(odd, pltpu.roll(first, HEAD_DIM, 1), first)
                right = jnp.where(odd, second, pltpu.roll(second, HEAD_DIM, 1))
                both = jnp.where(low, left, right)
                if part == 0:
                    both = both * (1.0 / math.sqrt(HEAD_DIM))
                start = part * WIDTH + pair * LANES
                outs[turn][:, start : start + LANES] = both.astype(jnp.bfloat16)


class Attention:
    def __init__(self, lengths_ref, place_ref):
        self.row_start = place_ref[0] * ROW
        self.y = place_ref[1]
        self.base = self.row_start - ROW
        self.ends = []
        total = jnp.int32(0)
        for j in range(UTTS):
            total = total + lengths_ref[0, j]
            self.ends.append(total)
        self.low = lax.broadcasted_iota(jnp.int32, (TOKENS, LANES), 1) < HEAD_DIM
        self.middle = lax.broadcasted_iota(jnp.int32, (2 * TOKENS, LANES), 1) == HEAD_DIM

    def steps_of(self, which):
        first = self.row_start + which * TOKENS
        last = first + TOKENS - 1
        begin = jnp.int32(0)
        finish = jnp.int32(0)
        for end in reversed(self.ends):
            finish = jnp.where(end > last, end, finish)
        for end in self.ends:
            begin = jnp.where(end <= first, end, begin)
        return lax.div(begin - self.base, CHUNK), lax.div(finish - self.base + CHUNK - 1, CHUNK)

    def segments(self, frames):
        found = jnp.zeros(frames.shape, jnp.int32)
        for end in self.ends:
            found = found + (frames >= end).astype(jnp.int32)
        return jnp.where(frames < 0, -1, found)

    def attend(self, which, queries, kv, step_of, count, scores, state, prior=None):
        low = self.low
        tops, totals, sums = (state.at[pl.ds(PAIRS * i, PAIRS)] for i in range(3))
        row_segment = self.segments(
            self.row_start + which * TOKENS + lax.broadcasted_iota(jnp.int32, (TOKENS, LANES), 0)
        )
        row_segment = jnp.concatenate([row_segment, row_segment], axis=1)
        stacked = []
        for pair in range(PAIRS):
            one = queries[pair]
            zero = jnp.zeros_like(one)
            stacked.append(
                jnp.concatenate([jnp.where(low, one, zero), jnp.where(low, zero, one)], axis=0)
            )
        tops[...] = jnp.full(tops.shape, masked_score, jnp.float32)

        def score(turn, carry):
            step, place = step_of(turn)
            start = pl.multiple_of(place * CHUNK, CHUNK)
            key_segment = self.segments(
                self.base + step * CHUNK + lax.broadcasted_iota(jnp.int32, (8, CHUNK), 1)
            )[:1]
            allowed = row_segment == key_segment
            allowed = jnp.concatenate([allowed, allowed], axis=0)
            for pair in range(PAIRS):
                keys = kv[pl.ds(start, CHUNK), pair * LANES : (pair + 1) * LANES]
                found = lax.dot_general(
                    stacked[pair], keys, (((1,), (1,)), ((), ())),
                    preferred_element_type=jnp.float32,
                )
                found = jnp.where(allowed, found, masked_score)
                scores[turn, pair] = found
                tops[pair] = jnp.maximum(
                    tops[pair], jnp.maximum(found[:, :LANES], found[:, LANES:])
                )
            return carry

        lax.fori_loop(0, count, score, 0)
        for pair in range(PAIRS):
            top = jnp.max(tops[pair], axis=1, keepdims=True)
            top = jnp.broadcast_to(top, (2 * TOKENS, LANES))
            if prior is None:
                tops[pair] = top
                totals[pair] = jnp.zeros((2 * TOKENS, LANES), jnp.float32)
                sums[pair] = jnp.zeros((2 * TOKENS, LANES), jnp.float32)
            else:
                stats = jnp.concatenate([prior[2 * pair], prior[2 * pair + 1]], axis=0)
                old = jnp.broadcast_to(stats[:, :1], (2 * TOKENS, LANES))
                top = jnp.maximum(top, old)
                tops[pair] = top
                factor = jnp.exp(old - top)
                totals[pair] = jnp.where(self.middle, stats * factor, 0.0)
                known = prior[2 * PAIRS + pair]
                sums[pair] = jnp.concatenate([known, known], axis=0) * factor

        def mix(turn, carry):
            _, place = step_of(turn)
            start = pl.multiple_of(place * CHUNK, CHUNK)
            for pair in range(PAIRS):
                found = scores[turn, pair]
                left = jnp.exp(found[:, :LANES] - tops[pair])
                right = jnp.exp(found[:, LANES:] - tops[pair])
                totals[pair] = totals[pair] + (left + right)
                weights = jnp.concatenate([left, right], axis=1).astype(jnp.bfloat16)
                values = kv[
                    pl.ds(start, CHUNK), WIDTH + pair * LANES : WIDTH + (pair + 1) * LANES
                ]
                sums[pair] = sums[pair] + jnp.dot(
                    weights, values, preferred_element_type=jnp.float32
                )
            return carry

        lax.fori_loop(0, count, mix, 0)


def local_kernel(lengths_ref, place_ref, own, next_piece, far, last, *rest):
    outs, (kv, queries, scores, state, packed, sems) = rest[:4], rest[4:]
    attention = Attention(lengths_ref, place_ref)
    pieces = (own, next_piece, far, last)
    asks, copies = [], []
    for turn in range(4):
        slot = lax.rem(attention.y + turn, 4)
        asks.append(
            pltpu.make_async_copy(
                pieces[turn].at[:, pl.ds(0, WIDTH)], queries.at[turn], sems.at[4 + turn]
            )
        )
        copies.append(
            pltpu.make_async_copy(
                pieces[turn].at[:, pl.ds(WIDTH, 2 * WIDTH)],
                kv.at[pl.ds(pl.multiple_of(slot * TOKENS, TOKENS), TOKENS)],
                sems.at[turn],
            )
        )
    for copy in asks + copies:
        copy.start()
    for copy in asks + copies:
        copy.wait()
    stores = []
    for i, offset in enumerate((2, 1, 3, 0)):
        which = lax.rem(attention.y + offset, 4)
        start, stop = attention.steps_of(which)
        start, stop = jnp.maximum(start, 2), jnp.minimum(stop, 4)
        asked = [queries[offset, :, pair * LANES : (pair + 1) * LANES] for pair in range(PAIRS)]
        attention.attend(
            which, asked, kv,
            lambda turn: (start + turn, start + turn - 2), stop - start,
            scores, state,
        )
        if i >= 2:
            stores[i - 2].wait()
        tiles = packed.at[i % 2]
        for pair in range(PAIRS):
            total = jnp.sum(state[PAIRS + pair], axis=1, keepdims=True)
            total = jnp.broadcast_to(total, (2 * TOKENS, LANES))
            top, found = state[pair], state[2 * PAIRS + pair]
            tiles[2 * pair] = jnp.where(attention.low, top[:TOKENS], total[:TOKENS])
            tiles[2 * pair + 1] = jnp.where(attention.low, top[TOKENS:], total[TOKENS:])
            tiles[2 * PAIRS + pair] = jnp.where(attention.low, found[:TOKENS], found[TOKENS:])
            tiles[3 * PAIRS + pair] = asked[pair].astype(jnp.float32)
        stores.append(pltpu.make_async_copy(tiles, outs[offset], sems.at[8 + i]))
        stores[i].start()
    stores[2].wait()
    stores[3].wait()


def project(mixed, core, own_weights, other_weights, store):
    for tile in range(8):
        high, place = divmod(tile, 4)
        both = jnp.concatenate([own_weights[place, high], other_weights[place, high]], axis=1)
        found = jnp.dot(mixed, both, preferred_element_type=jnp.float32)
        start = tile * 2 * LANES
        store(pl.multiple_of(start + core * LANES, LANES), found[:, :LANES])
        store(pl.multiple_of(start + (1 - core) * LANES, LANES), found[:, LANES:])


def attend_rows(offsets, lengths_ref, place_ref, before, after, priors, kv, scores, state, mixed, sems):
    attention = Attention(lengths_ref, place_ref)
    whiches, aheads, behinds = [], [], []
    for offset in offsets:
        which = lax.rem(attention.y + offset, 4)
        start, stop = attention.steps_of(which)
        whiches.append(which)
        aheads.append(jnp.maximum(2 - start, 0))
        behinds.append(jnp.maximum(stop - 4, 0))
    most_ahead = functools.reduce(jnp.maximum, aheads)
    most_behind = functools.reduce(jnp.maximum, behinds)
    copies = []
    for side, source in enumerate((before, after)):
        for turn in range(4):
            slot = lax.rem(attention.y + turn, 4)
            half = lax.div(slot, 2)
            copy = pltpu.make_async_copy(
                source.at[pl.ds(turn * TOKENS, TOKENS)],
                kv.at[pl.ds(pl.multiple_of((4 * side + slot) * TOKENS, TOKENS), TOKENS)],
                sems.at[4 * side + turn],
            )
            copies.append((half < most_behind if side else half >= 2 - most_ahead, copy))
    for wanted, copy in copies:
        @pl.when(wanted)
        def _():
            copy.start()
    for wanted, copy in copies:
        @pl.when(wanted)
        def _():
            copy.wait()
    for i, which in enumerate(whiches):
        ahead, behind, prior = aheads[i], behinds[i], priors[i]

        def step_of(turn):
            early = turn < ahead
            step = jnp.where(early, 2 - ahead + turn, 4 + turn - ahead)
            return step, jnp.where(early, step, step - 2)

        queries = [prior[3 * PAIRS + pair].astype(jnp.bfloat16) for pair in range(PAIRS)]
        attention.attend(which, queries, kv, step_of, ahead + behind, scores, state, prior)
        for pair in range(PAIRS):
            row_total = jnp.sum(state[PAIRS + pair], axis=1, keepdims=True)
            found = state[2 * PAIRS + pair] / row_total
            mixed[i * TOKENS : (i + 1) * TOKENS, pair * LANES : (pair + 1) * LANES] = jnp.where(
                attention.low, found[:TOKENS], found[TOKENS:]
            ).astype(jnp.bfloat16)


def attend_kernel(offsets, lengths_ref, place_ref, before, after, *rest):
    count = len(offsets)
    priors, (mixed, *scratch) = rest[:count], rest[count:]
    kv, scores, state, sems = scratch
    attend_rows(
        offsets, lengths_ref, place_ref, before, after, priors, kv, scores, state, mixed, sems
    )


def project_kernel(place_ref, own_weights, other_weights, mixed, out_ref):
    def store(start, value):
        out_ref[:, pl.ds(start, LANES)] = value.astype(out_ref.dtype)

    project(mixed[...], place_ref[2], own_weights, other_weights, store)


def rows_kernel(
    offsets, lengths_ref, place_ref, own_weights, other_weights, before, after, *rest
):
    count = len(offsets)
    priors, outs, scratch = rest[:count], rest[count : 2 * count], rest[2 * count :]
    kv, scores, state, sems, mixed = scratch
    attend_rows(
        offsets, lengths_ref, place_ref, before, after, priors, kv, scores, state, mixed, sems
    )

    def store(start, value):
        for i, out_ref in enumerate(outs):
            part = value[i * TOKENS : (i + 1) * TOKENS]
            out_ref[:, pl.ds(start, LANES)] = part.astype(out_ref.dtype)

    project(mixed[...], place_ref[2], own_weights, other_weights, store)


def finish_kernel(own_ref, one_ref, two_ref, three_ref, resid_ref, earlier_ref, out_hbm, out, sems):
    def deliver(step):
        rows = pl.ds(pl.multiple_of(step * PACKED, PACKED), PACKED)
        return pltpu.make_async_copy(out.at[rows], out_hbm.at[rows], sems.at[step])

    def finish(step, carry):
        rows = pl.ds(pl.multiple_of(step * PACKED, PACKED), PACKED)
        branch = own_ref[rows] + one_ref[rows].astype(jnp.float32)
        branch = branch + two_ref[rows].astype(jnp.float32)
        branch = branch + three_ref[rows].astype(jnp.float32)
        summed = resid_ref[rows].astype(jnp.float32) + branch * (1.0 / math.sqrt(D))
        centered = summed - jnp.mean(summed, axis=1, keepdims=True)
        spread = jnp.mean(centered * centered, axis=1, keepdims=True)
        normed = centered * lax.rsqrt(spread + norm_epsilon)
        out[rows] = (earlier_ref[rows] + normed) * (1.0 / TOP_K)
        deliver(step).start()
        return carry

    steps = TOKENS // PACKED
    lax.fori_loop(0, steps, finish, 0)
    for step in range(steps):
        deliver(step).wait()


vmem = pl.BlockSpec(memory_space=pltpu.VMEM)
smem = pl.BlockSpec(memory_space=pltpu.SMEM)
anywhere = pl.BlockSpec(memory_space=pl.ANY)
running = (3 * PAIRS, 2 * TOKENS, LANES)
handed = (4 * PAIRS, TOKENS, LANES)
local_scratch = [
    pltpu.VMEM((ROW, 2 * WIDTH), jnp.bfloat16),
    pltpu.VMEM((4, TOKENS, WIDTH), jnp.bfloat16),
    pltpu.VMEM((2, PAIRS, 2 * TOKENS, CHUNK), jnp.float32),
    pltpu.VMEM(running, jnp.float32),
    pltpu.VMEM((2,) + handed, jnp.float32),
    pltpu.SemaphoreType.DMA((12,)),
]
rows_scratch = [
    pltpu.VMEM((2 * ROW, 2 * WIDTH), jnp.bfloat16),
    pltpu.VMEM((4, PAIRS, 2 * TOKENS, CHUNK), jnp.float32),
    pltpu.VMEM(running, jnp.float32),
    pltpu.SemaphoreType.DMA((8,)),
]


def cost(flops, moved, exps=0):
    return pl.CostEstimate(flops=flops, bytes_accessed=moved, transcendentals=exps)


def limit(mebibytes):
    return pltpu.CompilerParams(vmem_limit_bytes=mebibytes << 20)


def array(*shape, dtype=jnp.bfloat16):
    return jax.ShapeDtypeStruct(shape, dtype)


def shift(value, amount, axis="y", size=4):
    return lax.ppermute(value, axis, [(i, (i + amount) % size) for i in range(size)])


def block(qkv, resid, earlier, lengths, teacher_out, student_out):
    teacher_new = (
        ema_decay * teacher_out.astype(jnp.float32)
        + (1.0 - ema_decay) * student_out.astype(jnp.float32)
    ).astype(jnp.bfloat16)
    place = jnp.stack([lax.axis_index(name) for name in ("z", "y", "c")]).astype(jnp.int32)

    pack = pl.pallas_call(
        pack_kernel,
        grid=(TOKENS // PACKED,),
        out_shape=(array(TOKENS, 3 * WIDTH),) * 4,
        in_specs=[smem, pl.BlockSpec((PACKED, 3 * D), lambda i: (i, 0))],
        out_specs=(pl.BlockSpec((PACKED, 3 * WIDTH), lambda i: (i, 0)),) * 4,
        compiler_params=limit(12),
        cost_estimate=cost(0, 3 << 20),
        name="pack",
    )
    packed = pack(place, qkv[0])

    pieces = [packed[0]]
    for turn in (1, 2, 3):
        pieces.append(shift(packed[turn], -turn))
    ring = 2 * lax.axis_size("z")
    keys = jnp.concatenate([piece[:, WIDTH:] for piece in pieces], axis=0)
    after = shift(keys, -1, ("h", "z"), ring)
    before = shift(keys, 1, ("h", "z"), ring)

    ring_weights = lax.all_to_all(
        jnp.broadcast_to(teacher_new[None], (16,) + teacher_new.shape), ("h", "z"), 0, 0, tiled=True
    )
    ring_weights = ring_weights.reshape(2, ROW, LANES)
    own_weights = lax.all_to_all(
        jnp.broadcast_to(ring_weights[None], (4,) + ring_weights.shape), "x", 0, 0, tiled=True
    )
    other_weights = shift(own_weights, 1, "c", 2)

    local = pl.pallas_call(
        local_kernel,
        out_shape=(array(*handed, dtype=jnp.float32),) * 4,
        in_specs=[smem, smem] + [anywhere] * 4,
        out_specs=(anywhere,) * 4,
        scratch_shapes=local_scratch,
        compiler_params=limit(LOCAL_LIMIT),
        cost_estimate=cost(1 << 30, 8 << 20, 2 << 20),
        name="local",
    )(lengths, place, *pieces)

    def rows_of(offsets, dtype):
        count = len(offsets)
        return pl.pallas_call(
            functools.partial(rows_kernel, offsets),
            out_shape=(array(TOKENS, D, dtype=dtype),) * count,
            in_specs=[smem, smem, vmem, vmem, anywhere, anywhere] + [vmem] * count,
            out_specs=(vmem,) * count,
            scratch_shapes=rows_scratch + [pltpu.VMEM((count * TOKENS, WIDTH), jnp.bfloat16)],
            compiler_params=limit(ROWS_LIMIT),
            cost_estimate=cost(count << 29, 4 << 20, count << 20),
            name="rows",
        )(
            lengths, place, own_weights, other_weights, before, after,
            *[local[offset] for offset in offsets],
        )

    mixed = pl.pallas_call(
        functools.partial(attend_kernel, (2,)),
        out_shape=array(TOKENS, WIDTH),
        in_specs=[smem, smem, anywhere, anywhere, vmem],
        out_specs=vmem,
        scratch_shapes=rows_scratch,
        compiler_params=limit(ROWS_LIMIT),
        cost_estimate=cost(1 << 28, 3 << 20, 1 << 20),
        name="attend",
    )(lengths, place, before, after, local[2])
    far = pl.pallas_call(
        project_kernel,
        out_shape=array(TOKENS, D),
        in_specs=[smem, vmem, vmem, vmem],
        out_specs=vmem,
        compiler_params=limit(8),
        cost_estimate=cost(2 * TOKENS * WIDTH * D, 3 << 20),
        name="project",
    )(place, own_weights, other_weights, mixed)
    far = shift(far, 2)
    up, down = rows_of((1, 3), jnp.bfloat16)
    up = shift(up, 1)
    down = shift(down, 3)
    (own,) = rows_of((0,), jnp.float32)
    targets = pl.pallas_call(
        finish_kernel,
        out_shape=array(TOKENS, D, dtype=jnp.float32),
        in_specs=[vmem] * 6,
        out_specs=anywhere,
        scratch_shapes=[
            pltpu.VMEM((TOKENS, D), jnp.float32),
            pltpu.SemaphoreType.DMA((TOKENS // PACKED,)),
        ],
        compiler_params=limit(12),
        cost_estimate=cost(1 << 22, 5 << 20),
        name="finish",
    )(own, far, up, down, resid[0], earlier[0])
    return (targets[None], teacher_new)


def solution(mesh):
    fine = Mesh(
        mesh.devices.reshape(2, 4, 2, 8, 4), ("h", "x", "c", "z", "y")
    )
    packs, frames = ("h", "x", "c"), ("z", "y")
    placed = (
        P(packs, frames, None),
        P(packs, frames, None),
        P(packs, frames, None),
        P(packs, None),
        P(frames, packs),
        P(frames, packs),
    )
    return jax.shard_map(
        block,
        mesh=fine,
        in_specs=placed,
        out_specs=(P(packs, frames, None), P(frames, packs)),
        check_vma=False,
    )
```
